32 devices in a mesh: dp: 8 (over y, x, core), tensor: 4 (over z).
Axes of the slice: x: 2, y: 2, z: 4, core: 2. Of those that a mesh axis runs over, the one named last changes fastest.
Arguments:
- image_in: bfloat16 [16, 1024, 1536], P('dp', None, 'tensor'), may hold values from -6 to 6
- text_in: bfloat16 [16, 154, 1536], P('dp', None, 'tensor'), may hold values from -6 to 6
- condition: bfloat16 [16, 1536], P('dp'), may hold values from -5 to 5
- image_cot: bfloat16 [16, 1024, 1536], P('dp', None, 'tensor'), may hold values from -6 to 6
- text_cot: bfloat16 [16, 154, 1536], P('dp', None, 'tensor'), may hold values from -6 to 6
- qkv_weight: bfloat16 [2, 1536, 3, 1536], P(None, 'dp', None, 'tensor'), may hold values from -0.15625 to 0.15625
- qv_bias: bfloat16 [2, 2, 1536], P(None, None, 'tensor'), may hold values from -3 to 3
- proj_weight: bfloat16 [2, 1536, 1536], P(None, 'tensor', 'dp'), may hold values from -2.5 to 2.5
- proj_bias: bfloat16 [2, 1536], P(None, 'tensor'), may hold values from -3 to 3
- up_weight: bfloat16 [2, 1536, 6144], P(None, 'dp', 'tensor'), may hold values from -0.15625 to 0.15625
- up_bias: bfloat16 [2, 6144], P(None, 'tensor'), may hold values from -3 to 3
- down_weight: bfloat16 [2, 6144, 1536], P(None, 'tensor', 'dp'), may hold values from -0.078125 to 0.078125
- down_bias: bfloat16 [2, 1536], P(None, 'tensor'), may hold values from -3 to 3
- mod_weight: bfloat16 [2, 1536, 6, 1536], P(None, 'dp', None, 'tensor'), may hold values from -0.15625 to 0.15625
- mod_bias: bfloat16 [2, 6, 1536], P(None, None, 'tensor'), may hold values from -3 to 3
Outputs:
- image_out: bfloat16 [16, 1024, 1536], P('dp', None, 'tensor')
- text_out: bfloat16 [16, 154, 1536], P('dp', None, 'tensor')
- image_grad: float32 [16, 1024, 1536], P('dp', None, 'tensor')
- text_grad: float32 [16, 154, 1536], P('dp', None, 'tensor')
- condition_grad: float32 [16, 1536], P('dp')
- qkv_weight_grad: float32 [2, 1536, 3, 1536], P(None, 'dp', None, 'tensor')
- qv_bias_grad: float32 [2, 2, 1536], P(None, None, 'tensor')
- proj_weight_grad: float32 [2, 1536, 1536], P(None, 'tensor', 'dp')
- proj_bias_grad: float32 [2, 1536], P(None, 'tensor')
- up_weight_grad: float32 [2, 1536, 6144], P(None, 'dp', 'tensor')
- up_bias_grad: float32 [2, 6144], P(None, 'tensor')
- down_weight_grad: float32 [2, 6144, 1536], P(None, 'tensor', 'dp')
- down_bias_grad: float32 [2, 1536], P(None, 'tensor')
- mod_weight_grad: float32 [2, 1536, 6, 1536], P(None, 'dp', None, 'tensor')
- mod_bias_grad: float32 [2, 6, 1536], P(None, None, 'tensor')
The draws below stay inside these ranges and needn't reach their ends.
All inputs are finite; a program needn't handle non-finite values.
Results may differ from the reference program's by a relative error of at most 0.017.
The reference program's roundings to bfloat16 on the way count: a program that leaves them out, or rounds other values in their place, can miss the bound.
Values may be sent and summed in bfloat16 or wider, within the bound.
No kernel may reach another device: no remote copies, remote signals or barrier semaphores. Data moves between devices by JAX's collectives and lax.ppermute only.
A program may use at most 176 MiB of HBM per device.

```python
import jax
import jax.numpy as jnp
from jax import lax

D = 1536
HEADS = 24
HEAD_DIM = 64
FF = 6144
IMG = 1024
TXT = 154
SAMPLES = 16


def levels(own_key, dims, split, least, high):
    level, own = 1.0, jax.random.fold_in(own_key, 6)
    for dim, parts in split:
        heights = jnp.exp(jax.random.uniform(jax.random.fold_in(own, dim), (parts,), jnp.float32, least / len(split), high / len(split)))
        level = level * jnp.repeat(heights, dims[dim] // parts).reshape([-1 if axis == dim else 1 for axis in range(len(dims))])
    return level


def centred(own_key, dims, scale, reach, split=(), held_as=jnp.bfloat16):
    values = scale * jax.random.normal(own_key, dims, jnp.float32)
    if split:
        values = values * levels(own_key, dims, split, -0.22, 0.18)
    return jnp.clip(values, -reach, reach).astype(held_as)


def setup_inputs(seed: int = 0) -> dict:
    keys = jax.random.split(jax.random.key(seed), 16)
    return {
        "image_in": centred(keys[0], (SAMPLES, IMG, D), 1.0, 6.0, ((0, 8), (2, 4))),
        "text_in": centred(keys[1], (SAMPLES, TXT, D), 1.0, 6.0, ((0, 8), (2, 4))),
        "condition": centred(keys[2], (SAMPLES, D), 1.0, 5.0, ((0, 8),)),
        "image_cot": centred(keys[3], (SAMPLES, IMG, D), 1.0, 6.0, ((0, 8), (2, 4))),
        "text_cot": centred(keys[4], (SAMPLES, TXT, D), 1.0, 6.0, ((0, 8), (2, 4))),
        "qkv_weight": centred(keys[5], (2, D, 3, D), D ** -0.5, 0.15625, ((1, 8), (3, 4))),
        "qv_bias": centred(keys[6], (2, 2, D), 0.5, 3.0, ((2, 4),)),
        "proj_weight": centred(keys[7], (2, D, D), (max(D // 256, 4)) ** -0.5, 2.5, ((1, 4), (2, 8))),
        "proj_bias": centred(keys[8], (2, D), 0.5, 3.0, ((1, 4),)),
        "up_weight": centred(keys[9], (2, D, FF), D ** -0.5, 0.15625, ((1, 8), (2, 4))),
        "up_bias": centred(keys[10], (2, FF), 0.5, 3.0, ((1, 4),)),
        "down_weight": centred(keys[11], (2, FF, D), FF ** -0.5, 0.078125, ((1, 4), (2, 8))),
        "down_bias": centred(keys[12], (2, D), 0.5, 3.0, ((1, 4),)),
        "mod_weight": centred(keys[13], (2, D, 6, D), D ** -0.5, 0.15625, ((1, 8), (3, 4))),
        "mod_bias": centred(keys[14], (2, 6, D), 0.5, 3.0, ((2, 4),)),
    }


@jax.custom_vjp
def low(v):
    return lax.optimization_barrier(v.astype(jnp.bfloat16)).astype(jnp.float32)

@jax.custom_vjp
def low_back(v):
    return v

def low_keep(v):
    return (low(v), None)

def low_pass(kept, grad):
    return (grad,)

def back_keep(v):
    return (v, None)

def back_low(kept, grad):
    return (low(grad),)
low.defvjp(low_keep, low_pass)
low_back.defvjp(back_keep, back_low)

def layer_norm(values):
    average = lax.optimization_barrier(jnp.mean(values, axis=-1, keepdims=True))
    spread = lax.optimization_barrier(jnp.mean(jnp.square(values - average), axis=-1, keepdims=True))
    return (values - average) * lax.rsqrt(spread + 1e-06)

def product(left_side, right_side):
    return jnp.dot(left_side, right_side, precision=lax.Precision.HIGHEST, preferred_element_type=jnp.float32)

def block_forward(image_rows, text_rows, condition_row, weights):
    qkv_weight, qv_bias, proj_weight, proj_bias, up_weight, up_bias, down_weight, down_bias, mod_weight, mod_bias = weights
    highest = lax.Precision.HIGHEST
    silu_cond = low(jax.nn.silu(condition_row))
    inputs = (image_rows, text_rows)
    modulations = []
    query_rows, key_rows, value_rows = ([], [], [])
    for modality in range(2):
        modulation = low_back(jnp.einsum('i,icj->cj', silu_cond, mod_weight[modality], precision=highest) + mod_bias[modality])
        modulations.append(modulation)
        attn_in = low(layer_norm(inputs[modality]) * (1.0 + modulation[1]) + modulation[0])
        projected = jnp.einsum('ni,icj->ncj', attn_in, qkv_weight[modality], precision=highest)
        query_rows.append(low(low_back(projected[:, 0] + qv_bias[modality, 0])))
        key_rows.append(low(low_back(projected[:, 1])))
        value_rows.append(low(low_back(projected[:, 2] + qv_bias[modality, 1])))
    length = IMG + TXT
    queries = jnp.concatenate(query_rows, 0).reshape(length, HEADS, HEAD_DIM)
    keys_joint = jnp.concatenate(key_rows, 0).reshape(length, HEADS, HEAD_DIM)
    values_joint = jnp.concatenate(value_rows, 0).reshape(length, HEADS, HEAD_DIM)
    scores = low_back(jnp.einsum('qhd,khd->hqk', queries, keys_joint, precision=highest) * HEAD_DIM ** (-0.5))
    probs_low = low(jax.nn.softmax(scores, axis=-1))
    attended = low(low_back(jnp.einsum('hqk,khd->qhd', probs_low, values_joint, precision=highest))).reshape(length, D)
    pieces = (attended[:IMG], attended[IMG:])
    results = []
    for modality in range(2):
        modulation = modulations[modality]
        branch_one = low_back(product(pieces[modality], proj_weight[modality]) + proj_bias[modality])
        middle = inputs[modality] + modulation[2] * branch_one
        mlp_in = low(layer_norm(middle) * (1.0 + modulation[4]) + modulation[3])
        pre_act = low_back(product(mlp_in, up_weight[modality]) + up_bias[modality])
        activated = low(jax.nn.gelu(pre_act, approximate=True))
        branch_two = low_back(product(activated, down_weight[modality]) + down_bias[modality])
        results.append(middle + modulation[5] * branch_two)
    return (results[0], results[1])

def reference(image_in, text_in, condition, image_cot, text_cot, qkv_weight, qv_bias, proj_weight, proj_bias, up_weight, up_bias, down_weight, down_bias, mod_weight, mod_bias):
    weights = tuple((tensor.astype(jnp.float32) for tensor in (qkv_weight, qv_bias, proj_weight, proj_bias, up_weight, up_bias, down_weight, down_bias, mod_weight, mod_bias)))

    def sample_step(totals, batch):
        image_rows, text_rows, condition_row, image_back, text_back = [entry.astype(jnp.float32) for entry in batch]
        outputs, pullback = jax.vjp(block_forward, image_rows, text_rows, condition_row, weights)
        grad_image, grad_text, grad_condition, grad_weights = pullback((image_back, text_back))
        totals = jax.tree.map(jnp.add, totals, grad_weights)
        return (totals, (outputs[0].astype(jnp.bfloat16), outputs[1].astype(jnp.bfloat16), grad_image, grad_text, grad_condition))
    start = jax.tree.map(jnp.zeros_like, weights)
    totals, stacked = lax.scan(sample_step, start, (image_in, text_in, condition, image_cot, text_cot))
    image_out, text_out, image_grad, text_grad, condition_grad = stacked
    qkv_grad, qv_grad, proj_grad, proj_bias_grad, up_grad, up_bias_grad, down_grad, down_bias_grad, mod_grad, mod_bias_grad = totals
    return (image_out, text_out, image_grad, text_grad, condition_grad, qkv_grad, qv_grad, proj_grad, proj_bias_grad, up_grad, up_bias_grad, down_grad, down_bias_grad, mod_grad, mod_bias_grad)
```

```python
import functools

import jax
import jax.numpy as jnp
from jax import lax
from jax.experimental import pallas as pl
from jax.experimental.pallas import tpu as pltpu
from jax.sharding import Mesh
from jax.sharding import PartitionSpec as P

D = 1536
HEAD_DIM = 64
NORM_EPS = 1e-06
GELU_SLOPE = (2.0 / 3.141592653589793) ** 0.5
GELU_CUBE = 0.044715
LOW = jnp.bfloat16
FULL = jnp.float32
SWAP = [(0, 1), (1, 0)]
BLOCK = 256
LANES = 128


def place():
    return lax.axis_index("core"), lax.axis_index("zp"), lax.axis_index("zl")


def ordered(first_here, here, there, axis):
    return jnp.where(
        first_here,
        jnp.concatenate([here, there], axis),
        jnp.concatenate([there, here], axis),
    )


def nn(left, right):
    return lax.dot_general(left, right, (((1,), (0,)), ((), ())), preferred_element_type=FULL)


def nt(left, right):
    return lax.dot_general(left, right, (((1,), (1,)), ((), ())), preferred_element_type=FULL)


def tn(left, right):
    return lax.dot_general(left, right, (((0,), (0,)), ((), ())), preferred_element_type=FULL)


def rows_call(kernel, name, image, rows, tiles, tables, outs, flops):
    split = image // BLOCK

    def by_rows(i, _):
        return (i, 0)

    def by_modality(i, _):
        return (jnp.minimum(i // split, 1), 0, 0)

    core = lax.axis_index("core").astype(jnp.int32).reshape(1)
    moved = sum(t.size * t.dtype.itemsize for t in (*tiles, *tables))
    moved += sum(rows * width * jnp.dtype(kind).itemsize for width, kind in outs)
    return pl.pallas_call(
        kernel,
        grid_spec=pltpu.PrefetchScalarGridSpec(
            num_scalar_prefetch=1,
            grid=(pl.cdiv(rows, BLOCK),),
            in_specs=[pl.BlockSpec((BLOCK, t.shape[1]), by_rows) for t in tiles]
            + [pl.BlockSpec((1, *t.shape[1:]), by_modality) for t in tables],
            out_specs=[pl.BlockSpec((BLOCK, width), by_rows) for width, _ in outs],
        ),
        out_shape=[jax.ShapeDtypeStruct((rows, width), kind) for width, kind in outs],
        compiler_params=pltpu.CompilerParams(
            dimension_semantics=("arbitrary",), vmem_limit_bytes=56 << 20
        ),
        cost_estimate=pl.CostEstimate(flops=flops, transcendentals=0, bytes_accessed=moved),
        name=name,
    )(core, *tiles, *tables)


def halves(core_ref, width):
    mine = pl.multiple_of(core_ref[0] * width, width)
    theirs = pl.multiple_of((1 - core_ref[0]) * width, width)
    return pl.ds(mine, width), pl.ds(theirs, width)


def qkv_kernel(core_ref, x_ref, mod_ref, w_ref, bias_ref, in_ref, out_ref, stat_ref):
    values = x_ref[...].astype(FULL)
    average = jnp.mean(values, axis=1, keepdims=True)
    centred = values - average
    factor = lax.rsqrt(jnp.mean(centred * centred, axis=1, keepdims=True) + NORM_EPS)
    shifted = (centred * factor * (1.0 + mod_ref[0, 1:2, :]) + mod_ref[0, 0:1, :]).astype(LOW)
    in_ref[...] = shifted
    out_ref[...] = (nn(shifted, w_ref[0]) + bias_ref[0]).astype(LOW)
    lane = lax.broadcasted_iota(jnp.int32, stat_ref.shape, 1)
    stat_ref[...] = jnp.where(lane == 0, average, factor)


def spread_kernel(core_ref, a_ref, w_ref, mine_ref, theirs_ref):
    mine, theirs = halves(core_ref, w_ref.shape[1] // 2)
    theirs_ref[...] = nt(a_ref[...], w_ref[0, theirs, :]).astype(LOW)
    mine_ref[...] = nt(a_ref[...], w_ref[0, mine, :]).astype(LOW)


def gather_kernel(core_ref, a_ref, w_ref, out_ref):
    out_ref[...] = nn(a_ref[...], w_ref[0]).astype(LOW)


def mlp_kernel(core_ref, a_ref, up_ref, bias_ref, down_ref, pre_ref, act_ref, mine_ref, theirs_ref):
    mine, theirs = halves(core_ref, down_ref.shape[1] // 2)
    pre = nn(a_ref[...], up_ref[0]) + bias_ref[0]
    pre_ref[...] = pre
    bent = jnp.tanh(GELU_SLOPE * (pre + GELU_CUBE * (pre * pre * pre)))
    act = (0.5 * pre * (1.0 + bent)).astype(LOW)
    act_ref[...] = act
    theirs_ref[...] = nt(act, down_ref[0, theirs, :]).astype(LOW)
    mine_ref[...] = nt(act, down_ref[0, mine, :]).astype(LOW)


def mlp_back_kernel(core_ref, g_ref, pre_ref, up_ref, down_ref, grad_ref, mine_ref, theirs_ref):
    mine, theirs = halves(core_ref, up_ref.shape[1] // 2)
    grad_act = nn(g_ref[...], down_ref[0])
    pre = pre_ref[...]
    square = pre * pre
    bent = jnp.tanh(GELU_SLOPE * pre * (1.0 + GELU_CUBE * square))
    slope = 0.5 * (1.0 + bent) + (0.5 * GELU_SLOPE) * pre * (1.0 - bent * bent) * (
        1.0 + (3.0 * GELU_CUBE) * square
    )
    grad = (grad_act * slope).astype(LOW)
    grad_ref[...] = grad
    theirs_ref[...] = nt(grad, up_ref[0, theirs, :]).astype(LOW)
    mine_ref[...] = nt(grad, up_ref[0, mine, :]).astype(LOW)


def weight_kernel(image, left_zero, left_one, right_zero, right_one, out_ref):
    for m, rows in enumerate((slice(0, image), slice(image, None))):
        out_ref[m] = (
            tn(left_zero[rows, :], right_zero[rows, :]) + tn(left_one[rows, :], right_one[rows, :])
        ).astype(LOW)


def weight_grad(image, lefts, rights):
    rows, width = lefts[0].shape
    across = rights[0].shape[1]
    return pl.pallas_call(
        functools.partial(weight_kernel, image),
        grid=(width // BLOCK,),
        in_specs=[pl.BlockSpec((rows, BLOCK), lambda i: (0, i))] * 2
        + [pl.BlockSpec((rows, across), lambda i: (0, 0))] * 2,
        out_specs=pl.BlockSpec((2, BLOCK, across), lambda i: (0, i, 0)),
        out_shape=jax.ShapeDtypeStruct((2, width, across), LOW),
        compiler_params=pltpu.CompilerParams(
            dimension_semantics=("arbitrary",), vmem_limit_bytes=56 << 20
        ),
        cost_estimate=pl.CostEstimate(
            flops=4 * rows * width * across,
            transcendentals=0,
            bytes_accessed=4 * (rows * (width + across) + width * across),
        ),
        name="weight_grad",
    )(*lefts, *rights)


def head_mask(values, head):
    lane = lax.broadcasted_iota(jnp.int32, values.shape, 1)
    return jnp.where((lane // HEAD_DIM) == head, values, jnp.zeros_like(values))


def live_rows(values, length):
    row = lax.broadcasted_iota(jnp.int32, values.shape, 0) + pl.program_id(1) * BLOCK
    return jnp.where(row < length, values, jnp.zeros_like(values))


def attend_kernel(length, q_ref, k_ref, v_ref, out_ref, log_ref, turned):
    @pl.when(pl.program_id(1) == 0)
    def _():
        turned[...] = v_ref[...].T

    queries = live_rows(q_ref[...], length) * jnp.asarray(HEAD_DIM**-0.5, LOW)
    keys_in = k_ref[...]
    cut = length // 8 * 8
    scores = [nt(keys_in, head_mask(queries, head)) for head in range(2)]
    found = []
    for head in range(2):
        row = lax.broadcasted_iota(jnp.int32, (keys_in.shape[0] - cut, BLOCK), 0)
        body = scores[head][:cut]
        tail = jnp.where(row < length - cut, scores[head][cut:], -1e30)
        highest = jnp.maximum(
            jnp.max(body, axis=0, keepdims=True), jnp.max(tail, axis=0, keepdims=True)
        )
        body, tail = jnp.exp(body - highest), jnp.exp(tail - highest)
        total = jnp.sum(body, axis=0, keepdims=True) + jnp.sum(tail, axis=0, keepdims=True)
        scale = 1.0 / total
        soft = jnp.concatenate([(body * scale).astype(LOW), (tail * scale).astype(LOW)], 0)
        found.append(nn(turned[head * HEAD_DIM : (head + 1) * HEAD_DIM, :], soft))
        log_ref[0, head : head + 1, :] = highest + jnp.log(total)
    out_ref[...] = jnp.concatenate(found, 0).T.astype(LOW)


def attend(joint, length):
    rows, width = joint.shape[0], joint.shape[1] // 3
    pairs, blocks = width // LANES, pl.cdiv(rows, BLOCK)
    area = 2 * pairs * rows * rows
    return pl.pallas_call(
        functools.partial(attend_kernel, length),
        out_shape=(
            jax.ShapeDtypeStruct((rows, width), LOW),
            jax.ShapeDtypeStruct((pairs, 8, blocks * BLOCK), FULL),
        ),
        grid=(pairs, blocks),
        in_specs=[
            pl.BlockSpec((BLOCK, LANES), lambda p, i: (i, p)),
            pl.BlockSpec((rows, LANES), lambda p, i: (0, pairs + p)),
            pl.BlockSpec((rows, LANES), lambda p, i: (0, 2 * pairs + p)),
        ],
        out_specs=(
            pl.BlockSpec((BLOCK, LANES), lambda p, i: (i, p)),
            pl.BlockSpec((1, 8, BLOCK), lambda p, i: (p, 0, i)),
        ),
        scratch_shapes=[pltpu.VMEM((LANES, rows), LOW)],
        compiler_params=pltpu.CompilerParams(
            dimension_semantics=("arbitrary", "arbitrary"), vmem_limit_bytes=56 << 20
        ),
        cost_estimate=pl.CostEstimate(
            flops=area * HEAD_DIM * 40, transcendentals=area, bytes_accessed=joint.size * 3
        ),
        name="attend",
    )(joint, joint, joint)


def attend_back_kernel(
    length, q_ref, k_ref, v_ref, up_ref, log_ref, out_ref, turned, key_sum, value_sum
):
    pair, block = pl.program_id(0), pl.program_id(1)
    pairs = pl.num_programs(0)

    @pl.when(block == 0)
    def _():
        turned[...] = k_ref[...].T
        key_sum[...] = jnp.zeros_like(key_sum)
        value_sum[...] = jnp.zeros_like(value_sum)

    rows = k_ref.shape[0]
    cut = length // 8 * 8
    scale = HEAD_DIM**-0.5
    queries = live_rows(q_ref[...], length) * jnp.asarray(scale, LOW)
    upstream = live_rows(up_ref[...], length)
    keys_in, values_in = k_ref[...], v_ref[...]
    masked = [head_mask(queries, head) for head in range(2)]
    above = [head_mask(upstream, head) for head in range(2)]
    scores, grad_soft = [], []
    for head in range(2):
        scores.append(nt(keys_in, masked[head]))
        grad_soft.append(nt(values_in, above[head]))
    row = lax.broadcasted_iota(jnp.int32, (rows - cut, BLOCK), 0)
    found = []
    for head in range(2):
        raised = jnp.exp(scores[head] - log_ref[0, head : head + 1, :])
        tail = jnp.where(row < length - cut, raised[cut:], 0.0)
        soft = jnp.concatenate([raised[:cut], tail], 0)
        inner = jnp.sum(soft * grad_soft[head], axis=0, keepdims=True)
        grad_scores = (soft * (grad_soft[head] - inner)).astype(LOW)
        value_sum[...] += nn(soft.astype(LOW), above[head])
        key_sum[...] += nn(grad_scores, masked[head])
        found.append(nn(turned[head * HEAD_DIM : (head + 1) * HEAD_DIM, :], grad_scores))
    first = pl.multiple_of(pair * LANES, LANES)
    start = pl.multiple_of(block * BLOCK, BLOCK)
    grad_queries = (jnp.concatenate(found, 0).T * scale).astype(LOW)
    last = pl.num_programs(1) - 1
    left = rows - rows // BLOCK * BLOCK

    @pl.when((block < last) if left else (block <= last))
    def _():
        out_ref[pl.ds(start, BLOCK), pl.ds(first, LANES)] = grad_queries

    if left:

        @pl.when(block == last)
        def _():
            out_ref[rows - left :, pl.ds(first, LANES)] = grad_queries[:left]

    @pl.when(block == last)
    def _():
        second = pl.multiple_of((pairs + pair) * LANES, LANES)
        third = pl.multiple_of((2 * pairs + pair) * LANES, LANES)
        out_ref[:, pl.ds(second, LANES)] = key_sum[...].astype(LOW)
        out_ref[:, pl.ds(third, LANES)] = value_sum[...].astype(LOW)


def attend_back(joint, log_total, upstream, length):
    rows, width = joint.shape[0], joint.shape[1] // 3
    pairs, blocks = width // LANES, pl.cdiv(rows, BLOCK)
    area = 2 * pairs * rows * rows
    return pl.pallas_call(
        functools.partial(attend_back_kernel, length),
        out_shape=jax.ShapeDtypeStruct((rows, 3 * width), LOW),
        grid=(pairs, blocks),
        in_specs=[
            pl.BlockSpec((BLOCK, LANES), lambda p, i: (i, p)),
            pl.BlockSpec((rows, LANES), lambda p, i: (0, pairs + p)),
            pl.BlockSpec((rows, LANES), lambda p, i: (0, 2 * pairs + p)),
            pl.BlockSpec((BLOCK, LANES), lambda p, i: (i, p)),
            pl.BlockSpec((1, 8, BLOCK), lambda p, i: (p, 0, i)),
        ],
        out_specs=pl.BlockSpec((rows, 3 * width), lambda p, i: (0, 0)),
        scratch_shapes=[
            pltpu.VMEM((LANES, rows), LOW),
            pltpu.VMEM((rows, LANES), FULL),
            pltpu.VMEM((rows, LANES), FULL),
        ],
        compiler_params=pltpu.CompilerParams(
            dimension_semantics=("arbitrary", "arbitrary"), vmem_limit_bytes=56 << 20
        ),
        cost_estimate=pl.CostEstimate(
            flops=area * HEAD_DIM * 60, transcendentals=area, bytes_accessed=joint.size * 6
        ),
        name="attend_back",
    )(joint, joint, joint, upstream, log_total)


def rehome(values):
    return lax.ppermute(values, ("core", "zp"), [(0, 0), (1, 2), (2, 1), (3, 3)])


def group_gather(own):
    core, _, near = place()
    half = ordered(near == 0, own, lax.ppermute(own, "zl", SWAP), own.ndim - 1)
    return ordered(core == 0, half, lax.ppermute(half, "core", SWAP), own.ndim - 1)


def group_reduce(mine, theirs):
    _, _, near = place()
    half = mine.astype(FULL) + lax.ppermute(theirs, "core", SWAP).astype(FULL)
    width = half.shape[1] // 2
    send = lax.dynamic_slice_in_dim(half, (1 - near) * width, width, 1).astype(LOW)
    own = lax.dynamic_slice_in_dim(half, near * width, width, 1)
    return own + lax.ppermute(send, "zl", SWAP).astype(FULL)


def group_sum(values):
    values = values + lax.ppermute(values, "core", SWAP)
    return values + lax.ppermute(values, "zl", SWAP)


def row_means(first, second):
    packed = group_sum(jnp.stack([first.sum(axis=1), (first * second).sum(axis=1)])) / D
    return packed[0][:, None], packed[1][:, None]


def weight_gather(shard):
    core, pair, _ = place()
    other = lax.ppermute(shard, "zp", SWAP)
    stays = core == pair
    keep = jnp.where(stays, shard, other)
    sibling = lax.ppermute(jnp.where(stays, other, shard), "core", SWAP)
    return lax.all_gather(ordered(core == 0, keep, sibling, 1), "yx", axis=1, tiled=True)


def weight_reduce(grad):
    core, pair, _ = place()
    block = lax.psum_scatter(grad, "yx", scatter_dimension=1, tiled=True)
    rows = block.shape[1] // 2
    keep = lax.dynamic_slice_in_dim(block, core * rows, rows, 1)
    sibling = lax.ppermute(
        lax.dynamic_slice_in_dim(block, (1 - core) * rows, rows, 1), "core", SWAP
    )
    stays = core == pair
    own = jnp.where(stays, keep, sibling)
    other = lax.ppermute(jnp.where(stays, sibling, keep), "zp", SWAP)
    return own.astype(FULL) + other.astype(FULL)


def steps(count):
    return [1 << bit for bit in range(count.bit_length() - 1)]


def dp_gather(values, planes):
    core = lax.axis_index("core")
    plane = lax.axis_index("yx")
    values = ordered(core == 0, values, lax.ppermute(values, "core", SWAP), 0)
    for bit in steps(planes):
        other = lax.ppermute(values, "yx", [(i, i ^ bit) for i in range(planes)])
        values = ordered((plane & bit) == 0, values, other, 0)
    return values


def dp_scatter_sum(values, planes):
    core = lax.axis_index("core")
    plane = lax.axis_index("yx")

    def halve(values, high, axis, perm):
        rows = values.shape[0] // 2
        send = lax.dynamic_slice_in_dim(values, (1 - high) * rows, rows, 0)
        keep = lax.dynamic_slice_in_dim(values, high * rows, rows, 0)
        return keep + lax.ppermute(send, axis, perm)

    for bit in reversed(steps(planes)):
        high = jnp.where((plane & bit) == 0, 0, 1)
        values = halve(values, high, "yx", [(i, i ^ bit) for i in range(planes)])
    return halve(values, core, "core", SWAP)


def mm(equation, left, right):
    return jnp.einsum(equation, left, right, preferred_element_type=FULL)


def per_device(
    planes,
    image_in,
    text_in,
    condition,
    image_cot,
    text_cot,
    qkv_weight,
    qv_bias,
    proj_weight,
    proj_bias,
    up_weight,
    up_bias,
    down_weight,
    down_bias,
    mod_weight,
    mod_bias,
):
    micro, image, quarter = image_in.shape
    text = text_in.shape[1]
    length = image + text
    rows = -(-length // 16) * 16
    core, pair, _ = place()
    stays = core == pair
    is_image = lax.broadcasted_iota(jnp.int32, (rows, 1), 0) < image

    def own_quarter(bias):
        bias = bias.astype(FULL)
        return jnp.where(stays, bias, rehome(bias))

    def join(image_part, text_part):
        return jnp.concatenate(
            [image_part, text_part, jnp.zeros((rows - length, image_part.shape[1]), LOW)], 0
        )

    def by_row(table):
        return jnp.where(is_image, table[0][None], table[1][None])

    def sums(values):
        values = values.astype(FULL)
        return jnp.stack([values[:image].sum(axis=0), values[image:].sum(axis=0)])

    inputs = [rehome(join(image_in[s], text_in[s])) for s in range(micro)]
    cotangents = [rehome(join(image_cot[s], text_cot[s])) for s in range(micro)]

    row_count = mod_weight.shape[1]
    cond_all = dp_gather(condition, planes)
    silu_all = jax.nn.silu(cond_all.astype(FULL)).astype(LOW)
    dp_index = lax.axis_index(("yx", "core"))
    silu_rows = lax.dynamic_slice_in_dim(silu_all, dp_index * row_count, row_count, 1)
    mod_terms = mm("bi,sicj->bscj", silu_rows, mod_weight)
    modulation = rehome(dp_scatter_sum(mod_terms, planes) + mod_bias.astype(FULL)[None])
    wide_modulation = group_gather(modulation[:, :, :2])

    qkv = weight_gather(qkv_weight.reshape(2, row_count, -1))
    proj = weight_gather(proj_weight.transpose(0, 2, 1))
    up = weight_gather(up_weight)
    down = weight_gather(down_weight.transpose(0, 2, 1))
    qv_own, proj_own, up_own, down_own = [
        own_quarter(bias) for bias in (qv_bias, proj_bias, up_bias, down_bias)
    ]
    qkv_own = jnp.concatenate([qv_own[:, 0], jnp.zeros_like(qv_own[:, 0]), qv_own[:, 1]], 1)
    call = functools.partial(rows_call, image=image, rows=rows)
    dense = 2 * rows * D

    outputs, input_grads, grad_mods, factors, bias_sums = [], [], [], [], []
    for s in range(micro):
        mod = modulation[s]
        wide = group_gather(inputs[s])
        residual = inputs[s].astype(FULL)
        attn_in, joint, stats = call(
            qkv_kernel,
            "qkv",
            tiles=[wide],
            tables=[wide_modulation[s], qkv, qkv_own[:, None]],
            outs=[(D, LOW), (3 * quarter, LOW), (LANES, FULL)],
            flops=dense * 3 * quarter,
        )
        normed_one = (residual - stats[:, 0:1]) * stats[:, 1:2]
        attended, log_total = attend(joint, length)
        reduced = group_reduce(
            *call(
                spread_kernel,
                "proj",
                tiles=[attended],
                tables=[proj],
                outs=[(D // 2, LOW), (D // 2, LOW)],
                flops=dense * quarter,
            )
        )
        branch_one = reduced + by_row(proj_own)
        middle = residual + by_row(mod[:, 2]) * branch_one
        average, square = row_means(middle, middle)
        factor_two = lax.rsqrt(square - average * average + NORM_EPS)
        normed_two = (middle - average) * factor_two
        mlp_in = group_gather(
            (normed_two * (1.0 + by_row(mod[:, 4])) + by_row(mod[:, 3])).astype(LOW)
        )
        hidden = up.shape[2]
        pre_act, activated, mine, theirs = call(
            mlp_kernel,
            "mlp",
            tiles=[mlp_in],
            tables=[up, up_own[:, None], down],
            outs=[(hidden, FULL), (hidden, LOW), (D // 2, LOW), (D // 2, LOW)],
            flops=dense * hidden * 2,
        )
        branch_two = group_reduce(mine, theirs) + by_row(down_own)
        outputs.append(rehome((middle + by_row(mod[:, 5]) * branch_two).astype(LOW)))

        upstream = cotangents[s].astype(FULL)
        grad_gate_two = sums(upstream * branch_two)
        grad_two = (by_row(mod[:, 5]) * upstream).astype(LOW)
        grad_two_full = group_gather(grad_two)
        grad_pre, mine, theirs = call(
            mlp_back_kernel,
            "mlp_back",
            tiles=[grad_two_full, pre_act],
            tables=[up, down],
            outs=[(hidden, LOW), (D // 2, LOW), (D // 2, LOW)],
            flops=dense * hidden * 2,
        )
        grad_mlp = group_reduce(mine, theirs)
        grad_shift_two = sums(grad_mlp)
        grad_scale_two = sums(grad_mlp * normed_two)
        scaled = grad_mlp * (1.0 + by_row(mod[:, 4]))
        grad_mean, cross_mean = row_means(scaled, normed_two)
        grad_middle = upstream + factor_two * (scaled - grad_mean - normed_two * cross_mean)
        grad_gate_one = sums(grad_middle * branch_one)
        grad_one = (by_row(mod[:, 2]) * grad_middle).astype(LOW)
        grad_one_full = group_gather(grad_one)
        (grad_attended,) = call(
            gather_kernel,
            "proj_back",
            tiles=[grad_one_full],
            tables=[proj],
            outs=[(quarter, LOW)],
            flops=dense * quarter,
        )
        grad_joint = attend_back(joint, log_total, grad_attended, length)
        grad_attn = group_reduce(
            *call(
                spread_kernel,
                "qkv_back",
                tiles=[grad_joint],
                tables=[qkv],
                outs=[(D // 2, LOW), (D // 2, LOW)],
                flops=dense * 3 * quarter,
            )
        )
        grad_shift_one = sums(grad_attn)
        grad_scale_one = sums(grad_attn * normed_one)
        scaled = grad_attn * (1.0 + by_row(mod[:, 1]))
        grad_mean, cross_mean = row_means(scaled, normed_one)
        grad_in = grad_middle + stats[:, 1:2] * (scaled - grad_mean - normed_one * cross_mean)
        input_grads.append(
            jnp.where(stays, grad_in, rehome(grad_in.astype(LOW)).astype(FULL))
        )
        grad_mods.append(
            jnp.stack(
                [
                    grad_shift_one,
                    grad_scale_one,
                    grad_gate_one,
                    grad_shift_two,
                    grad_scale_two,
                    grad_gate_two,
                ],
                1,
            )
        )
        grad_qkv_sums = sums(grad_joint)
        bias_sums.append(
            (
                jnp.stack([grad_qkv_sums[:, :quarter], grad_qkv_sums[:, 2 * quarter :]], 1),
                sums(grad_one),
                sums(grad_pre),
                sums(grad_two),
            )
        )
        factors.append(
            (
                (attn_in, grad_joint),
                (grad_one_full, attended),
                (mlp_in, grad_pre),
                (grad_two_full, activated),
            )
        )

    def reduced_grad(index):
        lefts, rights = zip(*[factor[index] for factor in factors])
        return weight_reduce(weight_grad(image, lefts, rights))

    down_grad = reduced_grad(3).transpose(0, 2, 1)
    up_grad = reduced_grad(2)
    proj_grad = reduced_grad(1).transpose(0, 2, 1)
    qkv_grad = reduced_grad(0).reshape(qkv_weight.shape)

    image_out = jnp.stack([output[:image] for output in outputs])
    text_out = jnp.stack([output[image:length] for output in outputs])
    image_grad = jnp.stack([grad[:image] for grad in input_grads])
    text_grad = jnp.stack([grad[image:length] for grad in input_grads])

    grad_mod_low = rehome(jnp.stack(grad_mods).astype(LOW))
    grad_mod_all = dp_gather(grad_mod_low, planes)
    mod_bias_grad = jnp.sum(grad_mod_all.astype(FULL), axis=0)
    mod_weight_grad = mm("bi,bscj->sicj", silu_rows, grad_mod_all)
    silu_grad_rows = mm("bscj,sicj->bi", grad_mod_all, mod_weight)
    silu_grad = lax.all_to_all(
        silu_grad_rows, ("yx", "core"), split_axis=0, concat_axis=1, tiled=True
    )
    silu_grad = silu_grad + lax.ppermute(silu_grad, "zp", SWAP)
    silu_grad = silu_grad + lax.ppermute(silu_grad, "zl", SWAP)
    condition_grad = jax.vjp(jax.nn.silu, condition.astype(FULL))[1](silu_grad)[0]

    totals = [sum(parts[1:], parts[0]) for parts in zip(*bias_sums)]
    packed = jnp.concatenate([total.reshape(-1) for total in totals])
    packed = packed + lax.ppermute(packed, "zp", SWAP)
    for bit in steps(planes):
        packed = packed + lax.ppermute(packed, "yx", [(i, i ^ bit) for i in range(planes)])
    packed = jnp.where(stays, packed, lax.ppermute(packed, "core", SWAP))
    bias_grads, start = [], 0
    for total in totals:
        bias_grads.append(packed[start : start + total.size].reshape(total.shape))
        start += total.size
    return (
        image_out,
        text_out,
        image_grad,
        text_grad,
        condition_grad,
        qkv_grad,
        bias_grads[0],
        proj_grad,
        bias_grads[1],
        up_grad,
        bias_grads[2],
        down_grad,
        bias_grads[3],
        mod_weight_grad,
        mod_bias_grad,
    )


def solution(mesh):
    planes = mesh.shape["dp"] // 2
    split = Mesh(mesh.devices.reshape(planes, 2, 2, 2), ("yx", "core", "zp", "zl"))
    dp, tensor = ("yx", "core"), ("zp", "zl")
    tokens = P(dp, None, tensor)
    placed = (
        tokens,
        tokens,
        P(dp, None),
        tokens,
        tokens,
        P(None, dp, None, tensor),
        P(None, None, tensor),
        P(None, tensor, dp),
        P(None, tensor),
        P(None, dp, tensor),
        P(None, tensor),
        P(None, tensor, dp),
        P(None, tensor),
        P(None, dp, None, tensor),
        P(None, None, tensor),
    )
    return jax.shard_map(
        functools.partial(per_device, planes),
        mesh=split,
        in_specs=placed,
        out_specs=(tokens,) * 4 + (P(dp, None),) + placed[5:],
        check_vma=False,
    )
```

```python
import functools

import jax
import jax.numpy as jnp
from jax import lax
from jax.experimental import pallas as pl
from jax.experimental.pallas import tpu as pltpu
from jax.sharding import Mesh
from jax.sharding import PartitionSpec as P

D = 1536
HEAD_DIM = 64
NORM_EPS = 1e-06
GELU_SLOPE = (2.0 / 3.141592653589793) ** 0.5
GELU_CUBE = 0.044715
LOW = jnp.bfloat16
FULL = jnp.float32
SWAP = [(0, 1), (1, 0)]
BLOCK = 256
ROWS = 512
LANES = 128


def place():
    return lax.axis_index("core"), lax.axis_index("zp"), lax.axis_index("zl")


def ordered(first_here, here, there, axis):
    return jnp.where(
        first_here,
        jnp.concatenate([here, there], axis),
        jnp.concatenate([there, here], axis),
    )


def nn(left, right):
    return lax.dot_general(left, right, (((1,), (0,)), ((), ())), preferred_element_type=FULL)


def nt(left, right):
    return lax.dot_general(left, right, (((1,), (1,)), ((), ())), preferred_element_type=FULL)


def tn(left, right):
    return lax.dot_general(left, right, (((0,), (0,)), ((), ())), preferred_element_type=FULL)


def rows_kernel(body, split, text, count, here_ref, *refs):
    def view(size):
        def cut(ref):
            return ref.at[pl.ds(0, size), :]

        tiles, tables, outs = refs[: count[0]], refs[count[0] : count[1]], refs[count[1] :]
        return (*map(cut, tiles), *tables, *map(cut, outs))

    @pl.when(pl.program_id(0) < split)
    def _():
        body(here_ref, *view(ROWS))

    @pl.when(pl.program_id(0) == split)
    def _():
        body(here_ref, *view(text))


def rows_call(kernel, name, image, rows, tiles, tables, outs, flops, scratch=()):
    split = image // ROWS

    def by_rows(i, _):
        return (i, 0)

    def by_modality(i, _):
        return (jnp.minimum(i // split, 1), 0, 0)

    here = jnp.stack([lax.axis_index("core"), lax.axis_index("zl")]).astype(jnp.int32)
    moved = sum(t.size * t.dtype.itemsize for t in (*tiles, *tables))
    moved += sum(rows * width * jnp.dtype(kind).itemsize for width, kind in outs)
    count = (len(tiles), len(tiles) + len(tables))
    return pl.pallas_call(
        functools.partial(rows_kernel, kernel, split, rows - image, count),
        grid_spec=pltpu.PrefetchScalarGridSpec(
            num_scalar_prefetch=1,
            grid=(split + 1,),
            in_specs=[pl.BlockSpec((ROWS, t.shape[1]), by_rows) for t in tiles]
            + [pl.BlockSpec((1, *t.shape[1:]), by_modality) for t in tables],
            out_specs=[pl.BlockSpec((ROWS, width), by_rows) for width, _ in outs],
            scratch_shapes=[pltpu.VMEM((ROWS, width), kind) for width, kind in scratch],
        ),
        out_shape=[jax.ShapeDtypeStruct((rows, width), kind) for width, kind in outs],
        compiler_params=pltpu.CompilerParams(
            dimension_semantics=("arbitrary",), vmem_limit_bytes=56 << 20
        ),
        cost_estimate=pl.CostEstimate(flops=flops, transcendentals=0, bytes_accessed=moved),
        name=name,
    )(here, *tiles, *tables)


def halves(here_ref, width):
    mine = pl.multiple_of(here_ref[0] * width, width)
    theirs = pl.multiple_of((1 - here_ref[0]) * width, width)
    return pl.ds(mine, width), pl.ds(theirs, width)


def gather_pieces(here_ref, pieces, full_ref):
    width = pieces[0].shape[1]
    for k, piece in enumerate(pieces):
        core = here_ref[0] if k < 2 else 1 - here_ref[0]
        near = here_ref[1] if k % 2 == 0 else 1 - here_ref[1]
        start = pl.multiple_of((2 * core + near) * width, LANES)
        full_ref[:, pl.ds(start, width)] = piece[...]


def spread(here_ref, value, read, outs):
    for refs, half in zip((outs[2:], outs[:2]), halves(here_ref, read.shape[1] // 2)[::-1]):
        found = nt(value, read[0, half, :]).astype(LOW)
        width = found.shape[1] // 2
        first, second = found[:, :width], found[:, width:]
        low = here_ref[1] == 0
        refs[0][...] = jnp.where(low, first, second)
        refs[1][...] = jnp.where(low, second, first)


def join_kernel(length, image_ref, text_ref, *outs):
    image, rows = image_ref.shape[1], outs[0].shape[0]
    start = length // 8 * 8
    for sample, out_ref in enumerate(outs):
        out_ref[:image, :] = image_ref[sample]
        out_ref[start:rows, :] = jnp.zeros((rows - start, out_ref.shape[1]), LOW)
        out_ref[image:length, :] = text_ref[sample]


def join(rows, image_part, text_part):
    samples, image, width = image_part.shape
    return pl.pallas_call(
        functools.partial(join_kernel, image + text_part.shape[1]),
        out_shape=[jax.ShapeDtypeStruct((rows, width), LOW)] * samples,
        compiler_params=pltpu.CompilerParams(vmem_limit_bytes=32 << 20),
        cost_estimate=pl.CostEstimate(
            flops=0, transcendentals=0, bytes_accessed=4 * samples * rows * width
        ),
        name="join",
    )(image_part, text_part)


def qkv_kernel(here_ref, *refs):
    pieces, (mod_ref, w_ref, bias_ref, in_ref, out_ref, stat_ref, full) = refs[:4], refs[4:]
    gather_pieces(here_ref, pieces, full)
    values = full[...].astype(FULL)
    average = jnp.mean(values, axis=1, keepdims=True)
    centred = values - average
    factor = lax.rsqrt(jnp.mean(centred * centred, axis=1, keepdims=True) + NORM_EPS)
    shifted = (centred * factor * (1.0 + mod_ref[0, 1:2, :]) + mod_ref[0, 0:1, :]).astype(LOW)
    in_ref[...] = shifted
    out_ref[...] = (nn(shifted, w_ref[0]) + bias_ref[0]).astype(LOW)
    lane = lax.broadcasted_iota(jnp.int32, stat_ref.shape, 1)
    stat_ref[...] = jnp.where(lane == 0, average, factor)


def spread_kernel(here_ref, a_ref, w_ref, *outs):
    spread(here_ref, a_ref[...], w_ref, outs)


def proj_back_kernel(here_ref, *refs):
    pieces, (w_ref, in_ref, out_ref) = refs[:4], refs[4:]
    gather_pieces(here_ref, pieces, in_ref)
    out_ref[...] = nn(in_ref[...], w_ref[0]).astype(LOW)


def gather_kernel(here_ref, *refs):
    gather_pieces(here_ref, refs[:4], refs[4])


def up_kernel(here_ref, *refs):
    pieces, (up_ref, bias_ref, in_ref, pre_ref, act_ref) = refs[:4], refs[4:]
    gather_pieces(here_ref, pieces, in_ref)
    values = in_ref[...]
    width = up_ref.shape[2] // 3
    for j in range(3):
        part = slice(j * width, (j + 1) * width)
        pre = nn(values, up_ref[0, :, part]) + bias_ref[0, :, part]
        pre_ref[:, part] = pre
        bent = jnp.tanh(GELU_SLOPE * (pre + GELU_CUBE * (pre * pre * pre)))
        act_ref[:, part] = (0.5 * pre * (1.0 + bent)).astype(LOW)


def mlp_back_kernel(here_ref, g_ref, pre_ref, up_ref, down_ref, grad_ref, *outs):
    values = g_ref[...]
    width = down_ref.shape[2] // 3
    for j in range(3):
        part = slice(j * width, (j + 1) * width)
        grad_act = nn(values, down_ref[0, :, part])
        pre = pre_ref[:, part]
        square = pre * pre
        bent = jnp.tanh(GELU_SLOPE * pre * (1.0 + GELU_CUBE * square))
        slope = 0.5 * (1.0 + bent) + (0.5 * GELU_SLOPE) * pre * (1.0 - bent * bent) * (
            1.0 + (3.0 * GELU_CUBE) * square
        )
        grad_ref[:, part] = (grad_act * slope).astype(LOW)
    spread(here_ref, grad_ref[...], up_ref, outs)


def weight_kernel(image, left_zero, left_one, right_zero, right_one, out_ref, sum_ref):
    for m, rows in enumerate((slice(0, image), slice(image, None))):
        out_ref[m] = (
            tn(left_zero[rows, :], right_zero[rows, :]) + tn(left_one[rows, :], right_one[rows, :])
        ).astype(LOW)

        @pl.when(pl.program_id(0) == 0)
        def _():
            sum_ref[m] = sum(
                jnp.sum(right[rows, :].astype(FULL), axis=0, keepdims=True)
                for right in (right_zero, right_one)
            )


def weight_grad(image, lefts, rights):
    rows, width = lefts[0].shape
    across = rights[0].shape[1]
    return pl.pallas_call(
        functools.partial(weight_kernel, image),
        grid=(width // BLOCK,),
        in_specs=[pl.BlockSpec((rows, BLOCK), lambda i: (0, i))] * 2
        + [pl.BlockSpec((rows, across), lambda i: (0, 0))] * 2,
        out_specs=[
            pl.BlockSpec((2, BLOCK, across), lambda i: (0, i, 0)),
            pl.BlockSpec((2, 1, across), lambda i: (0, 0, 0)),
        ],
        out_shape=[
            jax.ShapeDtypeStruct((2, width, across), LOW),
            jax.ShapeDtypeStruct((2, 1, across), FULL),
        ],
        compiler_params=pltpu.CompilerParams(
            dimension_semantics=("arbitrary",), vmem_limit_bytes=56 << 20
        ),
        cost_estimate=pl.CostEstimate(
            flops=4 * rows * width * across,
            transcendentals=0,
            bytes_accessed=4 * (rows * (width + across) + width * across),
        ),
        name="weight_grad",
    )(*lefts, *rights)


def head_mask(values, head):
    lane = lax.broadcasted_iota(jnp.int32, values.shape, 1)
    return jnp.where((lane // HEAD_DIM) == head, values, jnp.zeros_like(values))


def live_rows(values, length):
    row = lax.broadcasted_iota(jnp.int32, values.shape, 0) + pl.program_id(1) * BLOCK
    return jnp.where(row < length, values, jnp.zeros_like(values))


def attend_kernel(length, q_ref, k_ref, v_ref, out_ref, log_ref, turned):
    @pl.when(pl.program_id(1) == 0)
    def _():
        turned[...] = v_ref[...].T

    queries = live_rows(q_ref[...], length) * jnp.asarray(HEAD_DIM**-0.5, LOW)
    keys_in = k_ref[...]
    cut = length // 8 * 8
    scores = [nt(keys_in, head_mask(queries, head)) for head in range(2)]
    found = []
    for head in range(2):
        row = lax.broadcasted_iota(jnp.int32, (keys_in.shape[0] - cut, BLOCK), 0)
        body = scores[head][:cut]
        tail = jnp.where(row < length - cut, scores[head][cut:], -1e30)
        highest = jnp.maximum(
            jnp.max(body, axis=0, keepdims=True), jnp.max(tail, axis=0, keepdims=True)
        )
        body, tail = jnp.exp(body - highest), jnp.exp(tail - highest)
        total = jnp.sum(body, axis=0, keepdims=True) + jnp.sum(tail, axis=0, keepdims=True)
        scale = 1.0 / total
        soft = jnp.concatenate([(body * scale).astype(LOW), (tail * scale).astype(LOW)], 0)
        found.append(nn(turned[head * HEAD_DIM : (head + 1) * HEAD_DIM, :], soft))
        log_ref[0, head : head + 1, :] = highest + jnp.log(total)
    out_ref[...] = jnp.concatenate(found, 0).T.astype(LOW)


def attend(joint, length):
    rows, width = joint.shape[0], joint.shape[1] // 3
    pairs, blocks = width // LANES, pl.cdiv(rows, BLOCK)
    area = 2 * pairs * rows * rows
    return pl.pallas_call(
        functools.partial(attend_kernel, length),
        out_shape=(
            jax.ShapeDtypeStruct((rows, width), LOW),
            jax.ShapeDtypeStruct((pairs, 8, blocks * BLOCK), FULL),
        ),
        grid=(pairs, blocks),
        in_specs=[
            pl.BlockSpec((BLOCK, LANES), lambda p, i: (i, p)),
            pl.BlockSpec((rows, LANES), lambda p, i: (0, pairs + p)),
            pl.BlockSpec((rows, LANES), lambda p, i: (0, 2 * pairs + p)),
        ],
        out_specs=(
            pl.BlockSpec((BLOCK, LANES), lambda p, i: (i, p)),
            pl.BlockSpec((1, 8, BLOCK), lambda p, i: (p, 0, i)),
        ),
        scratch_shapes=[pltpu.VMEM((LANES, rows), LOW)],
        compiler_params=pltpu.CompilerParams(
            dimension_semantics=("arbitrary", "arbitrary"), vmem_limit_bytes=56 << 20
        ),
        cost_estimate=pl.CostEstimate(
            flops=area * HEAD_DIM * 40, transcendentals=area, bytes_accessed=joint.size * 3
        ),
        name="attend",
    )(joint, joint, joint)


def attend_back_kernel(
    length, q_ref, k_ref, v_ref, up_ref, log_ref, out_ref, turned, key_sum, value_sum
):
    pair, block = pl.program_id(0), pl.program_id(1)
    pairs = pl.num_programs(0)

    @pl.when(block == 0)
    def _():
        turned[...] = k_ref[...].T
        key_sum[...] = jnp.zeros_like(key_sum)
        value_sum[...] = jnp.zeros_like(value_sum)

    rows = k_ref.shape[0]
    cut = length // 8 * 8
    scale = HEAD_DIM**-0.5
    queries = live_rows(q_ref[...], length) * jnp.asarray(scale, LOW)
    upstream = live_rows(up_ref[...], length)
    keys_in, values_in = k_ref[...], v_ref[...]
    masked = [head_mask(queries, head) for head in range(2)]
    above = [head_mask(upstream, head) for head in range(2)]
    scores, grad_soft = [], []
    for head in range(2):
        scores.append(nt(keys_in, masked[head]))
        grad_soft.append(nt(values_in, above[head]))
    row = lax.broadcasted_iota(jnp.int32, (rows - cut, BLOCK), 0)
    found = []
    for head in range(2):
        raised = jnp.exp(scores[head] - log_ref[0, head : head + 1, :])
        tail = jnp.where(row < length - cut, raised[cut:], 0.0)
        soft = jnp.concatenate([raised[:cut], tail], 0)
        inner = jnp.sum(soft * grad_soft[head], axis=0, keepdims=True)
        grad_scores = (soft * (grad_soft[head] - inner)).astype(LOW)
        value_sum[...] += nn(soft.astype(LOW), above[head])
        key_sum[...] += nn(grad_scores, masked[head])
        found.append(nn(turned[head * HEAD_DIM : (head + 1) * HEAD_DIM, :], grad_scores))
    first = pl.multiple_of(pair * LANES, LANES)
    start = pl.multiple_of(block * BLOCK, BLOCK)
    grad_queries = (jnp.concatenate(found, 0).T * scale).astype(LOW)
    last = pl.num_programs(1) - 1
    left = rows - rows // BLOCK * BLOCK

    @pl.when((block < last) if left else (block <= last))
    def _():
        out_ref[pl.ds(start, BLOCK), pl.ds(first, LANES)] = grad_queries

    if left:

        @pl.when(block == last)
        def _():
            out_ref[rows - left :, pl.ds(first, LANES)] = grad_queries[:left]

    @pl.when(block == last)
    def _():
        second = pl.multiple_of((pairs + pair) * LANES, LANES)
        third = pl.multiple_of((2 * pairs + pair) * LANES, LANES)
        out_ref[:, pl.ds(second, LANES)] = key_sum[...].astype(LOW)
        out_ref[:, pl.ds(third, LANES)] = value_sum[...].astype(LOW)


def attend_back(joint, log_total, upstream, length):
    rows, width = joint.shape[0], joint.shape[1] // 3
    pairs, blocks = width // LANES, pl.cdiv(rows, BLOCK)
    area = 2 * pairs * rows * rows
    return pl.pallas_call(
        functools.partial(attend_back_kernel, length),
        out_shape=jax.ShapeDtypeStruct((rows, 3 * width), LOW),
        grid=(pairs, blocks),
        in_specs=[
            pl.BlockSpec((BLOCK, LANES), lambda p, i: (i, p)),
            pl.BlockSpec((rows, LANES), lambda p, i: (0, pairs + p)),
            pl.BlockSpec((rows, LANES), lambda p, i: (0, 2 * pairs + p)),
            pl.BlockSpec((BLOCK, LANES), lambda p, i: (i, p)),
            pl.BlockSpec((1, 8, BLOCK), lambda p, i: (p, 0, i)),
        ],
        out_specs=pl.BlockSpec((rows, 3 * width), lambda p, i: (0, 0)),
        scratch_shapes=[
            pltpu.VMEM((LANES, rows), LOW),
            pltpu.VMEM((rows, LANES), FULL),
            pltpu.VMEM((rows, LANES), FULL),
        ],
        compiler_params=pltpu.CompilerParams(
            dimension_semantics=("arbitrary", "arbitrary"), vmem_limit_bytes=56 << 20
        ),
        cost_estimate=pl.CostEstimate(
            flops=area * HEAD_DIM * 60, transcendentals=area, bytes_accessed=joint.size * 6
        ),
        name="attend_back",
    )(joint, joint, joint, upstream, log_total)


def settle_kernel(planes, plane_ref, *refs):
    *parts, out_ref = refs
    plane = plane_ref[0]
    blocks = planes // 2
    rows = parts[0].shape[0] // blocks
    for turned in range(2):
        high = (plane // blocks + turned) % 2
        start = pl.multiple_of(high * (blocks * rows), 8)
        out_ref[0, pl.ds(start, blocks * rows), :] = parts[turned][...]
        low = (plane + turned) % 2
        for b in range(blocks):
            turn = int(f"{b:0{max(blocks.bit_length() - 1, 1)}b}"[::-1], 2)
            start = pl.multiple_of((2 * turn + low) * rows, 8)
            out_ref[1, pl.ds(start, rows), :] = parts[2 + turned][b * rows : (b + 1) * rows, :]


def settle(planes, parts, there):
    rows, width = parts[0].shape
    plane = lax.axis_index("yx").astype(jnp.int32).reshape(1)
    return pl.pallas_call(
        functools.partial(settle_kernel, planes),
        in_specs=[pl.BlockSpec(memory_space=pltpu.SMEM)]
        + [pl.BlockSpec(memory_space=pltpu.VMEM)] * 4,
        out_specs=pl.BlockSpec(memory_space=pltpu.VMEM),
        out_shape=jax.ShapeDtypeStruct((2, 2 * rows, width), LOW),
        compiler_params=pltpu.CompilerParams(vmem_limit_bytes=40 << 20),
        cost_estimate=pl.CostEstimate(
            flops=0, transcendentals=0, bytes_accessed=16 * rows * width
        ),
        name="settle",
    )(plane, parts[0], there[0], parts[1], there[1])


class Line:
    def __init__(self):
        self.held, self.pending = (), []

    def due(self, steps_between, *values):
        self.pending.append((steps_between, values))

    def wait(self, *values):
        self.due(0, *values)

    def run(self, step, *operands):
        waits = [values for count, values in self.pending if count <= 0]
        self.pending = [(count - 1, values) for count, values in self.pending if count > 0]
        operands, _ = lax.optimization_barrier((operands, (self.held, waits)))
        results = step(*operands)
        self.held = tuple(jax.tree.leaves(results)[:1])
        return results


def apart(flag, step, *operands):
    shapes = jax.eval_shape(step, *operands)

    def skip(_):
        return jax.tree.map(lambda shape: jnp.zeros(shape.shape, shape.dtype), shapes)

    return lax.cond(flag, lambda values: step(*values), skip, operands)


def after(value, earlier):
    return lax.optimization_barrier((value, earlier))[0]


def away(values):
    return lax.ppermute(values, ("core", "zp"), [(1, 2), (2, 1)])


def rehome(values):
    core, pair, _ = place()
    return jnp.where(core == pair, values, away(values))


def over(axis, values):
    return lax.ppermute(values, axis, SWAP)


def over_planes(values, bit, planes):
    return lax.ppermute(values, "yx", [(i, i ^ bit) for i in range(planes)])


def group_gather(own):
    core, _, near = place()
    half = ordered(near == 0, own, over("zl", own), own.ndim - 1)
    return ordered(core == 0, half, over("core", half), own.ndim - 1)


def group_sum(values):
    values = values + over("core", values)
    return values + over("zl", values)


def steps(count):
    return [1 << bit for bit in range(count.bit_length() - 1)]


def dp_gather(values, planes):
    core = lax.axis_index("core")
    plane = lax.axis_index("yx")
    values = ordered(core == 0, values, over("core", values), 0)
    for bit in steps(planes):
        values = ordered((plane & bit) == 0, values, over_planes(values, bit, planes), 0)
    return values


def dp_scatter_sum(values, planes):
    core = lax.axis_index("core")
    plane = lax.axis_index("yx")

    def halve(values, high):
        rows = values.shape[0] // 2
        send = lax.dynamic_slice_in_dim(values, (1 - high) * rows, rows, 0)
        return lax.dynamic_slice_in_dim(values, high * rows, rows, 0), send

    for bit in reversed(steps(planes)):
        keep, send = halve(values, jnp.where((plane & bit) == 0, 0, 1))
        values = keep + over_planes(send, bit, planes)
    keep, send = halve(values, core)
    return keep + over("core", send)


class WeightGather:
    def __init__(self, line, shard, planes):
        self.line, self.shard, self.planes = line, shard, planes
        self.other = over("zp", shard)

    def swap(self):
        core, pair, _ = place()
        stays = core == pair
        self.keep, send = self.line.run(
            lambda a, b: (jnp.where(stays, a, b), jnp.where(stays, b, a)), self.shard, self.other
        )
        self.sibling = over("core", send)

    @staticmethod
    def whole(shard, other):
        core, pair, _ = place()
        keep = jnp.where(core == pair, shard, other)
        sibling = over("core", jnp.where(core == pair, other, shard))
        return ordered(core == 0, keep, sibling, 1)

    def block(self):
        core = lax.axis_index("core")
        return self.line.run(lambda a, b: ordered(core == 0, a, b, 1), self.keep, self.sibling)

    def offload(self):
        return lax.all_gather(self.block(), "yx", axis=1, tiled=True)

    def split(self):
        core = lax.axis_index("core")
        self.parts = self.line.run(
            lambda a, b: tuple(ordered(core == 0, a[m], b[m], 0) for m in range(2)),
            self.keep,
            self.sibling,
        )
        self.turn = 0
        self.send()

    def send(self):
        bits = steps(self.planes)
        self.bits = (bits[self.turn], bits[-1 - self.turn])
        self.there = [over_planes(p, b, self.planes) for p, b in zip(self.parts, self.bits)]
        self.turn += 1

    def grow(self):
        plane = lax.axis_index("yx")
        bits, count = self.bits, len(steps(self.planes))

        def step(here, there):
            return tuple(
                ordered((plane & b) == 0, h, t, 0) for h, t, b in zip(here, there, bits)
            )

        if self.turn == count:
            return self.line.run(
                functools.partial(settle, self.planes), self.parts, tuple(self.there)
            )
        self.parts = self.line.run(step, self.parts, self.there)
        self.send()

    def most(self):
        for _ in steps(self.planes)[1:]:
            self.grow()


class WeightReduce:
    def __init__(self, line, planes):
        self.line, self.planes = line, planes

    def offload(self, grad):
        self.part = lax.psum_scatter(grad, "yx", scatter_dimension=1, tiled=True)

    def split(self, grad):
        plane = lax.axis_index("yx")
        bits = steps(self.planes)
        count = len(bits)
        self.left = [bits[::-1], bits]

        def cut(values):
            return tuple(
                v.reshape(*[2] * count, v.shape[0] >> count, v.shape[1]) for v in values
            )

        self.cut = lambda values: tuple(
            self.halves(v, plane, m, self.left[m]) for m, v in enumerate(values)
        )
        self.kept = self.line.run(lambda g: self.cut(cut((g[0], g[1]))), grad)
        self.send()

    def halves(self, values, plane, m, left):
        axis = 0 if m == 0 else len(left) - 1
        high = jnp.where((plane & left[0]) == 0, 0, 1)
        return (
            lax.dynamic_index_in_dim(values, high, axis, keepdims=False),
            lax.dynamic_index_in_dim(values, 1 - high, axis, keepdims=False).astype(LOW),
        )

    def send(self):
        self.there = [
            over_planes(self.kept[m][1], self.left[m][0], self.planes) for m in range(2)
        ]

    def shrink(self):
        self.left = [left[1:] for left in self.left]

        def add(kept, there):
            return tuple(k[0].astype(FULL) + t.astype(FULL) for k, t in zip(kept, there))

        if self.left[0]:
            self.kept = self.line.run(lambda k, t: self.cut(add(k, t)), self.kept, self.there)
            self.send()
        else:
            self.part = (self.kept, self.there, add)

    def most(self):
        for _ in steps(self.planes)[1:]:
            self.shrink()

    def swap(self):
        core = lax.axis_index("core")

        def step(part):
            if isinstance(part, tuple):
                part = jnp.stack(part)
            part = part.astype(LOW)
            rows = part.shape[1] // 2
            return (
                lax.dynamic_slice_in_dim(part, core * rows, rows, 1),
                lax.dynamic_slice_in_dim(part, (1 - core) * rows, rows, 1),
            )

        if isinstance(self.part, tuple):
            kept, there, add = self.part
            self.keep, send = self.line.run(lambda k, t: step(add(k, t)), kept, there)
        else:
            self.keep, send = self.line.run(step, self.part)
        self.sibling = over("core", send)

    def hop(self):
        core, pair, _ = place()
        stays = core == pair
        self.own, send = self.line.run(
            lambda a, b: (jnp.where(stays, a, b), jnp.where(stays, b, a)), self.keep, self.sibling
        )
        self.other = over("zp", send)

    def cross(self):
        core = lax.axis_index("core")
        both = self.line.run(
            lambda a, b: jnp.where(core == 0, jnp.stack([a, b]), jnp.stack([b, a])),
            self.keep,
            self.sibling,
        )
        self.total = lax.psum_scatter(both, "zp", scatter_dimension=0, tiled=False)


def mm(equation, left, right):
    return jnp.einsum(equation, left, right, preferred_element_type=FULL)


def per_device(
    planes,
    image_in,
    text_in,
    condition,
    image_cot,
    text_cot,
    qkv_weight,
    qv_bias,
    proj_weight,
    proj_bias,
    up_weight,
    up_bias,
    down_weight,
    down_bias,
    mod_weight,
    mod_bias,
):
    micro, image, quarter = image_in.shape
    length = image + text_in.shape[1]
    rows = -(-length // 16) * 16
    both = range(micro)
    core, pair, near = place()
    stays = core == pair
    is_image = lax.broadcasted_iota(jnp.int32, (rows, 1), 0) < image
    line = Line()

    def own_quarter(bias):
        return rehome(bias.astype(FULL))

    def by_row(table):
        return jnp.where(is_image, table[0][None], table[1][None])

    def sums(values):
        values = values.astype(FULL)
        return jnp.stack([values[:image].sum(axis=0), values[image:].sum(axis=0)])

    def gather(own):
        other, far = over("zl", own), over("core", own)
        return own, other, far, over("core", other)

    def fold(parts):
        own, near, (own_there, near_there) = parts
        line.wait(own_there)
        send = line.run(
            lambda a, b: (a.astype(FULL) + b.astype(FULL)).astype(LOW), near, near_there
        )
        return own, own_there, over("zl", send)

    def total(part):
        return part[0].astype(FULL) + part[1].astype(FULL) + part[2].astype(FULL)

    def row_sums(first, second):
        return jnp.stack([first.sum(axis=1), (first * second).sum(axis=1)])

    def columns(totals):
        return totals[0][:, None] / D, totals[1][:, None] / D

    row_count = mod_weight.shape[1]
    shards = [
        qkv_weight.reshape(2, row_count, -1),
        proj_weight.transpose(0, 2, 1),
        up_weight,
        down_weight.transpose(0, 2, 1),
    ]
    qkv_way = WeightGather(line, shards[0], planes)

    cond_all = dp_gather(condition, planes)
    silu_all = jax.nn.silu(cond_all.astype(FULL)).astype(LOW)
    dp_index = lax.axis_index(("yx", "core"))
    silu_rows = lax.dynamic_slice_in_dim(silu_all, dp_index * row_count, row_count, 1)
    mod_terms = mm("bi,sicj->bscj", silu_rows, mod_weight)
    mod_local = dp_scatter_sum(mod_terms, planes) + mod_bias.astype(FULL)[None]
    modulation = rehome(mod_local)
    wide_modulation = group_gather(modulation[:, :, :2])
    qv_own, proj_own, up_own, down_own = [
        own_quarter(bias) for bias in (qv_bias, proj_bias, up_bias, down_bias)
    ]
    qkv_own = jnp.concatenate([qv_own[:, 0], jnp.zeros_like(qv_own[:, 0]), qv_own[:, 1]], 1)

    call = functools.partial(rows_call, image=image, rows=rows)
    dense = 2 * rows * D
    hidden = up_weight.shape[2]

    def qkv_step(s, pieces):
        return line.run(
            lambda a, b, c, d: call(
                qkv_kernel,
                "qkv",
                tiles=a,
                tables=[b, c, d],
                outs=[(D, LOW), (3 * quarter, LOW), (LANES, FULL)],
                flops=dense * 3 * quarter,
                scratch=[(D, LOW)],
            ),
            pieces,
            wide_modulation[s],
            qkv,
            qkv_own[:, None],
        )

    def parts_of(outs):
        own, near, own_theirs, near_theirs = outs
        far = over("core", near_theirs)
        return own, near, (over("core", own_theirs), far)

    def spread_step(name, value, weight):
        return parts_of(
            line.run(
                lambda a, b: call(
                    spread_kernel,
                    name,
                    tiles=[a],
                    tables=[b],
                    outs=[(quarter, LOW)] * 4,
                    flops=dense * value.shape[1],
                ),
                value,
                weight,
            )
        )

    def up_step(pieces):
        return line.run(
            lambda a, b, c: call(
                up_kernel,
                "up",
                tiles=a,
                tables=[b, c],
                outs=[(D, LOW), (hidden, FULL), (hidden, LOW)],
                flops=dense * hidden,
            ),
            pieces,
            up,
            up_own[:, None],
        )

    def gather_step(pieces):
        return line.run(
            lambda a: call(gather_kernel, "gather", tiles=a, tables=[], outs=[(D, LOW)], flops=0),
            pieces,
        )[0]

    def mlp_back_step(value, pre):
        grad, *outs = line.run(
            lambda a, b, c, d: call(
                mlp_back_kernel,
                "mlp_back",
                tiles=[a, b],
                tables=[c, d],
                outs=[(hidden, LOW)] + [(quarter, LOW)] * 4,
                flops=dense * hidden * 2,
            ),
            value,
            pre,
            up,
            down,
        )
        return grad, parts_of(outs)

    def proj_back_step(pieces):
        return line.run(
            lambda a, b: call(
                proj_back_kernel,
                "proj_back",
                tiles=a,
                tables=[b],
                outs=[(D, LOW), (quarter, LOW)],
                flops=dense * quarter,
            ),
            pieces,
            proj,
        )

    def grad_step(lefts, rights):
        return line.run(lambda a, b: weight_grad(image, a, b), tuple(lefts), tuple(rights))

    def middle_step(s, part):
        def step(part, x, mod, bias):
            branch = total(part) + by_row(bias)
            value = x.astype(FULL) + by_row(mod[:, 2]) * branch
            return row_sums(value, value), value, branch

        totals, value, branch = line.run(step, part, inputs[s], modulation[s], proj_own)
        return group_sum(totals), value, branch

    def second_norm(s, totals, value):
        def step(totals, value, mod):
            average, square = columns(totals)
            factor = lax.rsqrt(square - average * average + NORM_EPS)
            normed = (value - average) * factor
            shifted = (normed * (1.0 + by_row(mod[:, 4])) + by_row(mod[:, 3])).astype(LOW)
            return shifted, normed, factor

        shifted, normed, factor = line.run(step, totals, value, modulation[s])
        return gather(shifted), normed, factor

    def cot_step(s):
        def step(cot, mod):
            low = (by_row(mod[:, 5]) * cot.astype(FULL)).astype(LOW)
            return low, sums(low)

        low, bias = line.run(step, cotangents[s], modulation[s])
        return gather(low), bias

    def scaled_step(s, part, normed, which):
        def step(part, normed, mod):
            grad = total(part)
            scaled = grad * (1.0 + by_row(mod[:, which]))
            return row_sums(scaled, normed), scaled, sums(grad), sums(grad * normed)

        totals, scaled, shift, scale = line.run(step, part, normed, modulation[s])
        return group_sum(totals), scaled, shift, scale

    def middle_back(s, totals, scaled, normed, factor, branch):
        def step(totals, scaled, normed, factor, branch, cot, mod):
            grad_mean, cross_mean = columns(totals)
            grad = cot.astype(FULL) + factor * (scaled - grad_mean - normed * cross_mean)
            low = (by_row(mod[:, 2]) * grad).astype(LOW)
            return low, grad, sums(grad * branch), sums(low)

        low, grad, gate, bias = line.run(
            step, totals, scaled, normed, factor, branch, cotangents[s], modulation[s]
        )
        return gather(low), grad, gate, bias

    def first_back(totals, scaled, normed, stats, grad_middle):
        def step(totals, scaled, normed, stats, grad_middle):
            grad_mean, cross_mean = columns(totals)
            grad = grad_middle + stats[:, 1:2] * (scaled - grad_mean - normed * cross_mean)
            return grad.astype(LOW), grad

        low, grad = line.run(step, totals, scaled, normed, stats, grad_middle)
        return grad, away(low)

    def output_step(s, part, value):
        def step(part, value, cot, mod, bias):
            branch = total(part) + by_row(bias)
            out = (value + by_row(mod[:, 5]) * branch).astype(LOW)
            return out, sums(cot.astype(FULL) * branch)

        out, gate = line.run(step, part, value, cotangents[s], modulation[s], down_own)
        return (out, away(out)), gate

    def first_norm(s, stats):
        return line.run(
            lambda x, t: (x.astype(FULL) - t[:, 0:1]) * t[:, 1:2], inputs[s], stats
        )

    none = [None] * micro
    wide, attn_in, joint, stats, attended, log_total = (list(none) for _ in range(6))
    branch_one, middle, totals, normed_two, factor_two = (list(none) for _ in range(5))
    mlp_in, pre_act, activated, grad_two, grad_two_full = (list(none) for _ in range(5))
    grad_pre, part_a, part_b, part_c = (list(none) for _ in range(4))
    shift_two, scale_two, gate_two, shift_one, scale_one, gate_one = (list(none) for _ in range(6))
    scaled, grad_middle, one_bias, grad_one_full, grad_joint = (list(none) for _ in range(5))
    normed_one, outs, grad_in = (list(none) for _ in range(3))

    def settle_in(own, moved):
        return line.run(lambda a, b: jnp.where(stays, a, b), own, moved)

    two_bias, pieces, parts = list(none), list(none), list(none)

    raw = line.run(functools.partial(join, rows), image_in, text_in)
    qkv_way.swap()
    moved = away(after(raw[0], qkv_way.keep))
    qkv_way.split()
    line.wait(mod_local)
    inputs = [settle_in(raw[0], moved)]
    wide[0] = gather(inputs[0])
    proj_way = WeightGather(line, after(shards[1], inputs[0]), planes)
    qkv_way.most()
    proj_way.swap()
    up_way = WeightGather(line, after(shards[2], proj_way.keep), planes)
    proj_way.split()
    cot_raw = line.run(functools.partial(join, rows), image_cot, text_cot)
    line.wait(wide[0][1])
    qkv = qkv_way.grow()
    attn_in[0], joint[0], stats[0] = qkv_step(0, wide[0])
    up_way.swap()
    moved = away(after(raw[1], up_way.keep))
    up = up_way.offload()
    proj_way.most()
    attended[0], log_total[0] = line.run(lambda a: attend(a, length), joint[0])
    inputs.append(settle_in(raw[1], moved))
    wide[1] = gather(inputs[1])
    moved = away(after(cot_raw[0], inputs[1]))
    proj = proj_way.grow()
    part_a[0] = spread_step("proj", attended[0], proj)
    part_a[0] = fold(part_a[0])
    cotangents = [settle_in(cot_raw[0], moved)]
    down_way = WeightGather(line, after(shards[3], cotangents[0]), planes)
    attn_in[1], joint[1], stats[1] = qkv_step(1, wide[1])
    totals[0], middle[0], branch_one[0] = middle_step(0, part_a[0])
    attended[1], log_total[1] = line.run(lambda a: attend(a, length), joint[1])
    down_way.swap()
    down = down_way.offload()
    pieces[0], normed_two[0], factor_two[0] = second_norm(0, totals[0], middle[0])
    part_a[1] = spread_step("proj", attended[1], proj)
    normed_one[0] = first_norm(0, stats[0])
    normed_one[1] = first_norm(1, stats[1])
    line.wait(pieces[0][1])
    part_a[1] = fold(part_a[1])
    mlp_in[0], pre_act[0], activated[0] = up_step(pieces[0])
    totals[1], middle[1], branch_one[1] = middle_step(1, part_a[1])
    pieces[1], normed_two[1], factor_two[1] = second_norm(1, totals[1], middle[1])
    line.wait(pieces[1][1])
    grad_two[0], two_bias[0] = cot_step(0)
    moved = away(after(cot_raw[1], grad_two[0][0]))
    mlp_in[1], pre_act[1], activated[1] = up_step(pieces[1])
    cotangents.append(settle_in(cot_raw[1], moved))
    line.wait(grad_two[0][1])
    grad_two[1], two_bias[1] = cot_step(1)
    grad_two_full[0] = gather_step(grad_two[0])
    line.wait(grad_two[1][1])
    grad_two_full[1] = gather_step(grad_two[1])

    down_sum = WeightReduce(line, planes)
    down_sum.offload(grad_step(grad_two_full, activated)[0])
    grad_pre[0], part_b[0] = mlp_back_step(grad_two_full[0], pre_act[0])
    part_b[0] = fold(part_b[0])
    grad_pre[1], part_b[1] = mlp_back_step(grad_two_full[1], pre_act[1])
    totals[0], scaled[0], shift_two[0], scale_two[0] = scaled_step(0, part_b[0], normed_two[0], 4)
    up_sum = WeightReduce(line, planes)
    grad, up_rows = grad_step(mlp_in, grad_pre)
    up_sum.offload(grad)
    part_b[1] = fold(part_b[1])
    part_c[0] = spread_step("down", activated[0], down)
    pieces[0], grad_middle[0], gate_one[0], one_bias[0] = middle_back(
        0, totals[0], scaled[0], normed_two[0], factor_two[0], branch_one[0]
    )
    part_c[1] = spread_step("down", activated[1], down)
    line.wait(pieces[0][1])
    totals[1], scaled[1], shift_two[1], scale_two[1] = scaled_step(1, part_b[1], normed_two[1], 4)
    part_c[0] = fold(part_c[0])
    pieces[1], grad_middle[1], gate_one[1], one_bias[1] = middle_back(
        1, totals[1], scaled[1], normed_two[1], factor_two[1], branch_one[1]
    )
    down_sum.swap()
    grad_one_full[0], grad_attended = proj_back_step(pieces[0])
    outs[0], gate_two[0] = output_step(0, part_c[0], middle[0])
    line.wait(pieces[1][1])
    part_c[1] = fold(part_c[1])
    down_sum.cross()
    grad_joint[0] = line.run(
        lambda a, b, c: attend_back(a, b, c, length), joint[0], log_total[0], grad_attended
    )
    up_sum.swap()
    grad_one_full[1], grad_attended = proj_back_step(pieces[1])
    up_sum.cross()
    part_a[0] = spread_step("qkv_back", grad_joint[0], qkv)
    proj_sum = WeightReduce(line, planes)
    proj_sum.offload(grad_step(grad_one_full, attended)[0])
    part_a[0] = fold(part_a[0])
    grad_joint[1] = line.run(
        lambda a, b, c: attend_back(a, b, c, length), joint[1], log_total[1], grad_attended
    )
    down_grad = line.run(lambda a: a.astype(FULL).transpose(0, 2, 1), down_sum.total)
    part_a[1] = spread_step("qkv_back", grad_joint[1], qkv)
    totals[0], scaled[0], shift_one[0], scale_one[0] = scaled_step(0, part_a[0], normed_one[0], 1)
    part_a[1] = fold(part_a[1])
    qkv_sum = WeightReduce(line, planes)
    grad, qkv_rows = grad_step(attn_in, grad_joint)
    qkv_sum.split(grad)
    grad_in[0] = first_back(totals[0], scaled[0], normed_one[0], stats[0], grad_middle[0])
    outs[1], gate_two[1] = output_step(1, part_c[1], middle[1])

    def pack():
        qv = jnp.concatenate([qkv_rows[:, 0, :quarter], qkv_rows[:, 0, 2 * quarter :]], 1)
        return jnp.concatenate(
            [qv, one_bias[0] + one_bias[1], two_bias[0] + two_bias[1], up_rows[:, 0]], 1
        )

    def mod_rows(s):
        return jnp.concatenate(
            [shift_one[s], scale_one[s], gate_one[s], shift_two[s], scale_two[s], gate_two[s]], 1
        )

    packed = line.run(pack)
    up_grad = line.run(lambda a: a.astype(FULL), up_sum.total)
    line.wait(grad_in[0][1])
    qkv_sum.most()
    totals[1], scaled[1], shift_one[1], scale_one[1] = scaled_step(1, part_a[1], normed_one[1], 1)
    proj_sum.swap()
    grad_in[1] = first_back(totals[1], scaled[1], normed_one[1], stats[1], grad_middle[1])
    grad_mods = line.run(lambda: jnp.stack([mod_rows(s) for s in both]).astype(LOW))
    line.wait(outs[1][1])
    grad_mods = line.run(rehome, grad_mods)
    qkv_sum.shrink()
    qkv_sum.swap()
    qkv_sum.hop()
    proj_sum.hop()

    def late(outs):
        outs = [jnp.where(stays, own, home) for own, home in outs]
        return (
            jnp.stack([out[:image] for out in outs]),
            jnp.stack([out[image:length] for out in outs]),
        )

    image_out, text_out = line.run(late, outs)

    def last_sums(grad_mods, packed, silu_rows, mod_weight, condition):
        every = dp_gather(grad_mods, planes)
        every = every.reshape(*every.shape[:2], 6, quarter)
        silu_grad = mm("bscj,sicj->bi", every, mod_weight)
        silu_grad = lax.all_to_all(
            silu_grad, ("yx", "core"), split_axis=0, concat_axis=1, tiled=True
        )
        for bit in steps(planes):
            packed = packed + over_planes(packed, bit, planes)
        packed = after(packed, silu_grad)
        packed = packed + over("zp", packed)
        packed = jnp.where(stays, packed, over("core", packed))
        silu_grad = silu_grad + over("zp", silu_grad)
        silu_grad = silu_grad + over("zl", silu_grad)
        return (
            jax.vjp(jax.nn.silu, condition.astype(FULL))[1](silu_grad)[0],
            mm("bi,bscj->sicj", silu_rows, every),
            jnp.sum(every.astype(FULL), axis=0),
            packed,
        )

    flag = condition[0, 0] == condition[0, 0]
    condition_grad, mod_weight_grad, mod_bias_grad, packed = line.run(
        functools.partial(apart, flag, last_sums),
        grad_mods,
        packed,
        silu_rows,
        mod_weight,
        condition,
    )
    qkv_grad, proj_grad = line.run(
        lambda sums: [own.astype(FULL) + other.astype(FULL) for own, other in sums],
        [(one.own, one.other) for one in (qkv_sum, proj_sum)],
    )
    qkv_grad = qkv_grad.reshape(qkv_weight.shape)
    bias_grads = [
        packed[:, : 2 * quarter].reshape(qv_bias.shape),
        packed[:, 2 * quarter : 3 * quarter],
        packed[:, 4 * quarter :],
        packed[:, 3 * quarter : 4 * quarter],
    ]

    grad_in = [jnp.where(stays, own, home.astype(FULL)) for own, home in grad_in]
    image_grad = jnp.stack([grad[:image] for grad in grad_in])
    text_grad = jnp.stack([grad[image:length] for grad in grad_in])
    proj_grad = proj_grad.transpose(0, 2, 1)
    return (
        image_out,
        text_out,
        image_grad,
        text_grad,
        condition_grad,
        qkv_grad,
        bias_grads[0],
        proj_grad,
        bias_grads[1],
        up_grad,
        bias_grads[2],
        down_grad,
        bias_grads[3],
        mod_weight_grad,
        mod_bias_grad,
    )


def solution(mesh):
    planes = mesh.shape["dp"] // 2
    split = Mesh(mesh.devices.reshape(planes, 2, 2, 2), ("yx", "core", "zp", "zl"))
    dp, tensor = ("yx", "core"), ("zp", "zl")
    tokens = P(dp, None, tensor)
    placed = (
        tokens,
        tokens,
        P(dp, None),
        tokens,
        tokens,
        P(None, dp, None, tensor),
        P(None, None, tensor),
        P(None, tensor, dp),
        P(None, tensor),
        P(None, dp, tensor),
        P(None, tensor),
        P(None, tensor, dp),
        P(None, tensor),
        P(None, dp, None, tensor),
        P(None, None, tensor),
    )
    return jax.shard_map(
        functools.partial(per_device, planes),
        mesh=split,
        in_specs=placed,
        out_specs=(tokens,) * 4 + (P(dp, None),) + placed[5:],
        check_vma=False,
    )
```

```python
import functools

import jax
import jax.numpy as jnp
from jax import lax
from jax.experimental import pallas as pl
from jax.experimental.pallas import tpu as pltpu
from jax.sharding import Mesh
from jax.sharding import PartitionSpec as P

D = 1536
HEAD_DIM = 64
NORM_EPS = 1e-06
GELU_SLOPE = (2.0 / 3.141592653589793) ** 0.5
GELU_CUBE = 0.044715
LOW = jnp.bfloat16
FULL = jnp.float32
SWAP = [(0, 1), (1, 0)]
BLOCK = 256
ROWS = 512
FORWARD = 1280
BACKWARD = 256
LANES = 128


def place():
    return lax.axis_index("core"), lax.axis_index("zp"), lax.axis_index("zl")


def ordered(first_here, here, there, axis):
    return jnp.where(
        first_here,
        jnp.concatenate([here, there], axis),
        jnp.concatenate([there, here], axis),
    )


def nn(left, right):
    return lax.dot_general(left, right, (((1,), (0,)), ((), ())), preferred_element_type=FULL)


def nt(left, right):
    return lax.dot_general(left, right, (((1,), (1,)), ((), ())), preferred_element_type=FULL)


def tn(left, right):
    return lax.dot_general(left, right, (((0,), (0,)), ((), ())), preferred_element_type=FULL)


def rows_kernel(body, split, text, count, here_ref, *refs):
    def view(size):
        def cut(ref):
            return ref.at[pl.ds(0, size), :]

        tiles, tables, outs = refs[: count[0]], refs[count[0] : count[1]], refs[count[1] :]
        return (*map(cut, tiles), *tables, *map(cut, outs))

    @pl.when(pl.program_id(0) < split)
    def _():
        body(here_ref, *view(ROWS))

    @pl.when(pl.program_id(0) == split)
    def _():
        body(here_ref, *view(text))


def rows_call(kernel, name, image, rows, tiles, tables, outs, flops, scratch=()):
    split = image // ROWS

    def by_rows(i, _):
        return (i, 0)

    def by_modality(i, _):
        return (jnp.minimum(i // split, 1), 0, 0)

    here = jnp.stack([lax.axis_index("core"), lax.axis_index("zl")]).astype(jnp.int32)
    moved = sum(t.size * t.dtype.itemsize for t in (*tiles, *tables))
    moved += sum(rows * width * jnp.dtype(kind).itemsize for width, kind in outs)
    count = (len(tiles), len(tiles) + len(tables))
    return pl.pallas_call(
        functools.partial(rows_kernel, kernel, split, rows - image, count),
        grid_spec=pltpu.PrefetchScalarGridSpec(
            num_scalar_prefetch=1,
            grid=(split + 1,),
            in_specs=[pl.BlockSpec((ROWS, t.shape[1]), by_rows) for t in tiles]
            + [pl.BlockSpec((1, *t.shape[1:]), by_modality) for t in tables],
            out_specs=[pl.BlockSpec((ROWS, width), by_rows) for width, _ in outs],
            scratch_shapes=[pltpu.VMEM((ROWS, width), kind) for width, kind in scratch],
        ),
        out_shape=[jax.ShapeDtypeStruct((rows, width), kind) for width, kind in outs],
        compiler_params=pltpu.CompilerParams(
            dimension_semantics=("arbitrary",), vmem_limit_bytes=56 << 20
        ),
        cost_estimate=pl.CostEstimate(flops=flops, transcendentals=0, bytes_accessed=moved),
        name=name,
    )(here, *tiles, *tables)


def halves(here_ref, width):
    mine = pl.multiple_of(here_ref[0] * width, width)
    theirs = pl.multiple_of((1 - here_ref[0]) * width, width)
    return pl.ds(mine, width), pl.ds(theirs, width)


def gather_pieces(here_ref, pieces, full_ref):
    width = pieces[0].shape[1]
    for k, piece in enumerate(pieces):
        core = here_ref[0] if k < 2 else 1 - here_ref[0]
        near = here_ref[1] if k % 2 == 0 else 1 - here_ref[1]
        start = pl.multiple_of((2 * core + near) * width, LANES)
        full_ref[:, pl.ds(start, width)] = piece[...]


def spread(here_ref, value, read, outs):
    for refs, half in zip((outs[2:], outs[:2]), halves(here_ref, read.shape[1] // 2)[::-1]):
        found = nt(value, read[0, half, :]).astype(LOW)
        width = found.shape[1] // 2
        first, second = found[:, :width], found[:, width:]
        low = here_ref[1] == 0
        refs[0][...] = jnp.where(low, first, second)
        refs[1][...] = jnp.where(low, second, first)


def join_kernel(length, image_ref, text_ref, *outs):
    image, rows = image_ref.shape[1], outs[0].shape[0]
    start = length // 8 * 8
    for sample, out_ref in enumerate(outs):
        out_ref[:image, :] = image_ref[sample]
        out_ref[start:rows, :] = jnp.zeros((rows - start, out_ref.shape[1]), LOW)
        out_ref[image:length, :] = text_ref[sample]


def join(rows, image_part, text_part):
    samples, image, width = image_part.shape
    return pl.pallas_call(
        functools.partial(join_kernel, image + text_part.shape[1]),
        out_shape=[jax.ShapeDtypeStruct((rows, width), LOW)] * samples,
        compiler_params=pltpu.CompilerParams(vmem_limit_bytes=32 << 20),
        cost_estimate=pl.CostEstimate(
            flops=0, transcendentals=0, bytes_accessed=4 * samples * rows * width
        ),
        name="join",
    )(image_part, text_part)


def qkv_kernel(here_ref, *refs):
    pieces, (mod_ref, w_ref, bias_ref, in_ref, out_ref, stat_ref, full) = refs[:4], refs[4:]
    gather_pieces(here_ref, pieces, full)
    values = full[...].astype(FULL)
    average = jnp.mean(values, axis=1, keepdims=True)
    centred = values - average
    factor = lax.rsqrt(jnp.mean(centred * centred, axis=1, keepdims=True) + NORM_EPS)
    shifted = (centred * factor * (1.0 + mod_ref[0, 1:2, :]) + mod_ref[0, 0:1, :]).astype(LOW)
    in_ref[...] = shifted
    out_ref[...] = (nn(shifted, w_ref[0]) + bias_ref[0]).astype(LOW)
    lane = lax.broadcasted_iota(jnp.int32, stat_ref.shape, 1)
    stat_ref[...] = jnp.where(lane == 0, average, factor)


def spread_kernel(here_ref, a_ref, w_ref, *outs):
    spread(here_ref, a_ref[...], w_ref, outs)


def proj_back_kernel(here_ref, *refs):
    pieces, (w_ref, in_ref, out_ref) = refs[:4], refs[4:]
    gather_pieces(here_ref, pieces, in_ref)
    out_ref[...] = nn(in_ref[...], w_ref[0]).astype(LOW)


def gather_kernel(here_ref, *refs):
    gather_pieces(here_ref, refs[:4], refs[4])


def up_kernel(here_ref, *refs):
    pieces, (up_ref, bias_ref, in_ref, pre_ref, act_ref) = refs[:4], refs[4:]
    gather_pieces(here_ref, pieces, in_ref)
    values = in_ref[...]
    width = up_ref.shape[2] // 3
    for j in range(3):
        part = slice(j * width, (j + 1) * width)
        pre = nn(values, up_ref[0, :, part]) + bias_ref[0, :, part]
        pre_ref[:, part] = pre
        bent = jnp.tanh(GELU_SLOPE * (pre + GELU_CUBE * (pre * pre * pre)))
        act_ref[:, part] = (0.5 * pre * (1.0 + bent)).astype(LOW)


def mlp_back_kernel(here_ref, g_ref, pre_ref, up_ref, down_ref, grad_ref, *outs):
    values = g_ref[...]
    width = down_ref.shape[2] // 3
    for j in range(3):
        part = slice(j * width, (j + 1) * width)
        grad_act = nn(values, down_ref[0, :, part])
        pre = pre_ref[:, part]
        square = pre * pre
        bent = jnp.tanh(GELU_SLOPE * pre * (1.0 + GELU_CUBE * square))
        slope = 0.5 * (1.0 + bent) + (0.5 * GELU_SLOPE) * pre * (1.0 - bent * bent) * (
            1.0 + (3.0 * GELU_CUBE) * square
        )
        grad_ref[:, part] = (grad_act * slope).astype(LOW)
    spread(here_ref, grad_ref[...], up_ref, outs)


def weight_kernel(image, left_zero, left_one, right_zero, right_one, out_ref, sum_ref):
    for m, rows in enumerate((slice(0, image), slice(image, None))):
        out_ref[m] = (
            tn(left_zero[rows, :], right_zero[rows, :]) + tn(left_one[rows, :], right_one[rows, :])
        ).astype(LOW)

        @pl.when(pl.program_id(0) == 0)
        def _():
            sum_ref[m] = sum(
                jnp.sum(right[rows, :].astype(FULL), axis=0, keepdims=True)
                for right in (right_zero, right_one)
            )


def weight_grad(image, lefts, rights):
    rows, width = lefts[0].shape
    across = rights[0].shape[1]
    return pl.pallas_call(
        functools.partial(weight_kernel, image),
        grid=(width // BLOCK,),
        in_specs=[pl.BlockSpec((rows, BLOCK), lambda i: (0, i))] * 2
        + [pl.BlockSpec((rows, across), lambda i: (0, 0))] * 2,
        out_specs=[
            pl.BlockSpec((2, BLOCK, across), lambda i: (0, i, 0)),
            pl.BlockSpec((2, 1, across), lambda i: (0, 0, 0)),
        ],
        out_shape=[
            jax.ShapeDtypeStruct((2, width, across), LOW),
            jax.ShapeDtypeStruct((2, 1, across), FULL),
        ],
        compiler_params=pltpu.CompilerParams(
            dimension_semantics=("arbitrary",), vmem_limit_bytes=56 << 20
        ),
        cost_estimate=pl.CostEstimate(
            flops=4 * rows * width * across,
            transcendentals=0,
            bytes_accessed=4 * (rows * (width + across) + width * across),
        ),
        name="weight_grad",
    )(*lefts, *rights)


def head_mask(values, head):
    lane = lax.broadcasted_iota(jnp.int32, values.shape, 1)
    return jnp.where((lane // HEAD_DIM) == head, values, jnp.zeros_like(values))


def live_rows(values, length):
    row = lax.broadcasted_iota(jnp.int32, values.shape, 0) + pl.program_id(1) * values.shape[0]
    return jnp.where(row < length, values, jnp.zeros_like(values))


def attend_kernel(length, q_ref, k_ref, v_ref, out_ref, log_ref, turned):
    @pl.when(pl.program_id(1) == 0)
    def _():
        turned[...] = v_ref[...].T

    queries = live_rows(q_ref[...], length) * jnp.asarray(HEAD_DIM**-0.5, LOW)
    keys_in = k_ref[...]
    cut = length // 8 * 8
    scores = [nt(keys_in, head_mask(queries, head)) for head in range(2)]
    found = []
    for head in range(2):
        row = lax.broadcasted_iota(jnp.int32, (keys_in.shape[0] - cut, FORWARD), 0)
        body = scores[head][:cut]
        tail = jnp.where(row < length - cut, scores[head][cut:], -1e30)
        highest = jnp.maximum(
            jnp.max(body, axis=0, keepdims=True), jnp.max(tail, axis=0, keepdims=True)
        )
        body, tail = jnp.exp(body - highest), jnp.exp(tail - highest)
        total = jnp.sum(body, axis=0, keepdims=True) + jnp.sum(tail, axis=0, keepdims=True)
        scale = 1.0 / total
        soft = jnp.concatenate([(body * scale).astype(LOW), (tail * scale).astype(LOW)], 0)
        found.append(nn(turned[head * HEAD_DIM : (head + 1) * HEAD_DIM, :], soft))
        log_ref[0, head : head + 1, :] = highest + jnp.log(total)
    out_ref[...] = jnp.concatenate(found, 0).T.astype(LOW)


def attend(joint, length):
    rows, width = joint.shape[0], joint.shape[1] // 3
    pairs, blocks = width // LANES, pl.cdiv(rows, FORWARD)
    area = 2 * pairs * rows * rows
    return pl.pallas_call(
        functools.partial(attend_kernel, length),
        out_shape=(
            jax.ShapeDtypeStruct((rows, width), LOW),
            jax.ShapeDtypeStruct((pairs, 8, blocks * FORWARD), FULL),
        ),
        grid=(pairs, blocks),
        in_specs=[
            pl.BlockSpec((FORWARD, LANES), lambda p, i: (i, p)),
            pl.BlockSpec((rows, LANES), lambda p, i: (0, pairs + p)),
            pl.BlockSpec((rows, LANES), lambda p, i: (0, 2 * pairs + p)),
        ],
        out_specs=(
            pl.BlockSpec((FORWARD, LANES), lambda p, i: (i, p)),
            pl.BlockSpec((1, 8, FORWARD), lambda p, i: (p, 0, i)),
        ),
        scratch_shapes=[pltpu.VMEM((LANES, rows), LOW)],
        compiler_params=pltpu.CompilerParams(
            dimension_semantics=("arbitrary", "arbitrary"), vmem_limit_bytes=56 << 20
        ),
        cost_estimate=pl.CostEstimate(
            flops=area * HEAD_DIM * 40, transcendentals=area, bytes_accessed=joint.size * 3
        ),
        name="attend",
    )(joint, joint, joint)


def attend_back_kernel(
    length, q_ref, k_ref, v_ref, up_ref, log_ref, out_ref, turned, key_sum, value_sum
):
    pair, block = pl.program_id(0), pl.program_id(1)
    pairs = pl.num_programs(0)

    @pl.when(block == 0)
    def _():
        turned[...] = k_ref[...].T
        key_sum[...] = jnp.zeros_like(key_sum)
        value_sum[...] = jnp.zeros_like(value_sum)

    rows = k_ref.shape[0]
    cut = length // 8 * 8
    scale = HEAD_DIM**-0.5
    queries = live_rows(q_ref[...], length) * jnp.asarray(scale, LOW)
    upstream = live_rows(up_ref[...], length)
    keys_in, values_in = k_ref[...], v_ref[...]
    masked = [head_mask(queries, head) for head in range(2)]
    above = [head_mask(upstream, head) for head in range(2)]
    scores, grad_soft = [], []
    for head in range(2):
        scores.append(nt(keys_in, masked[head]))
        grad_soft.append(nt(values_in, above[head]))
    row = lax.broadcasted_iota(jnp.int32, (rows - cut, BACKWARD), 0)
    found = []
    for head in range(2):
        raised = jnp.exp(scores[head] - log_ref[0, head : head + 1, :])
        tail = jnp.where(row < length - cut, raised[cut:], 0.0)
        soft = jnp.concatenate([raised[:cut], tail], 0)
        inner = jnp.sum(soft * grad_soft[head], axis=0, keepdims=True)
        grad_scores = (soft * (grad_soft[head] - inner)).astype(LOW)
        value_sum[...] += nn(soft.astype(LOW), above[head])
        key_sum[...] += nn(grad_scores, masked[head])
        found.append(nn(turned[head * HEAD_DIM : (head + 1) * HEAD_DIM, :], grad_scores))
    first = pl.multiple_of(pair * LANES, LANES)
    start = pl.multiple_of(block * BACKWARD, BACKWARD)
    grad_queries = (jnp.concatenate(found, 0).T * scale).astype(LOW)
    last = pl.num_programs(1) - 1
    left = rows - rows // BACKWARD * BACKWARD

    @pl.when((block < last) if left else (block <= last))
    def _():
        out_ref[pl.ds(start, BACKWARD), pl.ds(first, LANES)] = grad_queries

    if left:

        @pl.when(block == last)
        def _():
            out_ref[rows - left :, pl.ds(first, LANES)] = grad_queries[:left]

    @pl.when(block == last)
    def _():
        second = pl.multiple_of((pairs + pair) * LANES, LANES)
        third = pl.multiple_of((2 * pairs + pair) * LANES, LANES)
        out_ref[:, pl.ds(second, LANES)] = key_sum[...].astype(LOW)
        out_ref[:, pl.ds(third, LANES)] = value_sum[...].astype(LOW)


def attend_back(joint, log_total, upstream, length):
    rows, width = joint.shape[0], joint.shape[1] // 3
    pairs, blocks = width // LANES, pl.cdiv(rows, BACKWARD)
    area = 2 * pairs * rows * rows
    return pl.pallas_call(
        functools.partial(attend_back_kernel, length),
        out_shape=jax.ShapeDtypeStruct((rows, 3 * width), LOW),
        grid=(pairs, blocks),
        in_specs=[
            pl.BlockSpec((BACKWARD, LANES), lambda p, i: (i, p)),
            pl.BlockSpec((rows, LANES), lambda p, i: (0, pairs + p)),
            pl.BlockSpec((rows, LANES), lambda p, i: (0, 2 * pairs + p)),
            pl.BlockSpec((BACKWARD, LANES), lambda p, i: (i, p)),
            pl.BlockSpec((1, 8, BACKWARD), lambda p, i: (p, 0, i)),
        ],
        out_specs=pl.BlockSpec((rows, 3 * width), lambda p, i: (0, 0)),
        scratch_shapes=[
            pltpu.VMEM((LANES, rows), LOW),
            pltpu.VMEM((rows, LANES), FULL),
            pltpu.VMEM((rows, LANES), FULL),
        ],
        compiler_params=pltpu.CompilerParams(
            dimension_semantics=("arbitrary", "arbitrary"), vmem_limit_bytes=56 << 20
        ),
        cost_estimate=pl.CostEstimate(
            flops=area * HEAD_DIM * 60, transcendentals=area, bytes_accessed=joint.size * 6
        ),
        name="attend_back",
    )(joint, joint, joint, upstream, log_total)


def settle_kernel(planes, plane_ref, *refs):
    *parts, out_ref = refs
    plane = plane_ref[0]
    blocks = planes // 2
    rows = parts[0].shape[0] // blocks
    for turned in range(2):
        high = (plane // blocks + turned) % 2
        start = pl.multiple_of(high * (blocks * rows), 8)
        out_ref[0, pl.ds(start, blocks * rows), :] = parts[turned][...]
        low = (plane + turned) % 2
        for b in range(blocks):
            turn = int(f"{b:0{max(blocks.bit_length() - 1, 1)}b}"[::-1], 2)
            start = pl.multiple_of((2 * turn + low) * rows, 8)
            out_ref[1, pl.ds(start, rows), :] = parts[2 + turned][b * rows : (b + 1) * rows, :]


def settle(planes, parts, there):
    rows, width = parts[0].shape
    plane = lax.axis_index("yx").astype(jnp.int32).reshape(1)
    return pl.pallas_call(
        functools.partial(settle_kernel, planes),
        in_specs=[pl.BlockSpec(memory_space=pltpu.SMEM)]
        + [pl.BlockSpec(memory_space=pltpu.VMEM)] * 4,
        out_specs=pl.BlockSpec(memory_space=pltpu.VMEM),
        out_shape=jax.ShapeDtypeStruct((2, 2 * rows, width), LOW),
        compiler_params=pltpu.CompilerParams(vmem_limit_bytes=40 << 20),
        cost_estimate=pl.CostEstimate(
            flops=0, transcendentals=0, bytes_accessed=16 * rows * width
        ),
        name="settle",
    )(plane, parts[0], there[0], parts[1], there[1])


class Line:
    def __init__(self):
        self.held, self.pending = (), []

    def due(self, steps_between, *values):
        self.pending.append((steps_between, values))

    def wait(self, *values):
        self.due(0, *values)

    def run(self, step, *operands):
        waits = [values for count, values in self.pending if count <= 0]
        self.pending = [(count - 1, values) for count, values in self.pending if count > 0]
        operands, _ = lax.optimization_barrier((operands, (self.held, waits)))
        results = step(*operands)
        self.held = tuple(jax.tree.leaves(results)[:1])
        return results


def apart(flag, step, *operands):
    shapes = jax.eval_shape(step, *operands)

    def skip(_):
        return jax.tree.map(lambda shape: jnp.zeros(shape.shape, shape.dtype), shapes)

    return lax.cond(flag, lambda values: step(*values), skip, operands)


def after(value, earlier):
    return lax.optimization_barrier((value, earlier))[0]


def away(values):
    return lax.ppermute(values, ("core", "zp"), [(1, 2), (2, 1)])


def rehome(values):
    core, pair, _ = place()
    return jnp.where(core == pair, values, away(values))


def over(axis, values):
    return lax.ppermute(values, axis, SWAP)


def over_planes(values, bit, planes):
    return lax.ppermute(values, "yx", [(i, i ^ bit) for i in range(planes)])


def group_gather(own):
    core, _, near = place()
    half = ordered(near == 0, own, over("zl", own), own.ndim - 1)
    return ordered(core == 0, half, over("core", half), own.ndim - 1)


def group_sum(values):
    values = values + over("core", values)
    return values + over("zl", values)


def steps(count):
    return [1 << bit for bit in range(count.bit_length() - 1)]


def dp_gather(values, planes):
    core = lax.axis_index("core")
    plane = lax.axis_index("yx")
    values = ordered(core == 0, values, over("core", values), 0)
    for bit in steps(planes):
        values = ordered((plane & bit) == 0, values, over_planes(values, bit, planes), 0)
    return values


def dp_scatter_sum(values, planes):
    core = lax.axis_index("core")
    plane = lax.axis_index("yx")

    def halve(values, high):
        rows = values.shape[0] // 2
        send = lax.dynamic_slice_in_dim(values, (1 - high) * rows, rows, 0)
        return lax.dynamic_slice_in_dim(values, high * rows, rows, 0), send

    for bit in reversed(steps(planes)):
        keep, send = halve(values, jnp.where((plane & bit) == 0, 0, 1))
        values = keep + over_planes(send, bit, planes)
    keep, send = halve(values, core)
    return keep + over("core", send)


class WeightGather:
    def __init__(self, line, shard, planes):
        self.line, self.shard, self.planes = line, shard, planes
        self.other = over("zp", shard)

    def swap(self):
        core, pair, _ = place()
        stays = core == pair
        self.keep, send = self.line.run(
            lambda a, b: (jnp.where(stays, a, b), jnp.where(stays, b, a)), self.shard, self.other
        )
        self.sibling = over("core", send)

    @staticmethod
    def whole(shard, other):
        core, pair, _ = place()
        keep = jnp.where(core == pair, shard, other)
        sibling = over("core", jnp.where(core == pair, other, shard))
        return ordered(core == 0, keep, sibling, 1)

    def block(self):
        core = lax.axis_index("core")
        return self.line.run(lambda a, b: ordered(core == 0, a, b, 1), self.keep, self.sibling)

    def offload(self):
        return lax.all_gather(self.block(), "yx", axis=1, tiled=True)

    def split(self):
        core = lax.axis_index("core")
        self.parts = self.line.run(
            lambda a, b: tuple(ordered(core == 0, a[m], b[m], 0) for m in range(2)),
            self.keep,
            self.sibling,
        )
        self.turn = 0
        self.send()

    def send(self):
        bits = steps(self.planes)
        self.bits = (bits[self.turn], bits[-1 - self.turn])
        self.there = [over_planes(p, b, self.planes) for p, b in zip(self.parts, self.bits)]
        self.turn += 1

    def grow(self):
        plane = lax.axis_index("yx")
        bits, count = self.bits, len(steps(self.planes))

        def step(here, there):
            return tuple(
                ordered((plane & b) == 0, h, t, 0) for h, t, b in zip(here, there, bits)
            )

        if self.turn == count:
            return self.line.run(
                functools.partial(settle, self.planes), self.parts, tuple(self.there)
            )
        self.parts = self.line.run(step, self.parts, self.there)
        self.send()

    def most(self):
        for _ in steps(self.planes)[1:]:
            self.grow()


class WeightReduce:
    def __init__(self, line, planes):
        self.line, self.planes = line, planes

    def offload(self, grad):
        self.part = lax.psum_scatter(grad, "yx", scatter_dimension=1, tiled=True)

    def split(self, grad):
        plane = lax.axis_index("yx")
        bits = steps(self.planes)
        count = len(bits)
        self.left = [bits[::-1], bits]

        def cut(values):
            return tuple(
                v.reshape(*[2] * count, v.shape[0] >> count, v.shape[1]) for v in values
            )

        self.cut = lambda values: tuple(
            self.halves(v, plane, m, self.left[m]) for m, v in enumerate(values)
        )
        self.kept = self.line.run(lambda g: self.cut(cut((g[0], g[1]))), grad)
        self.send()

    def halves(self, values, plane, m, left):
        axis = 0 if m == 0 else len(left) - 1
        high = jnp.where((plane & left[0]) == 0, 0, 1)
        return (
            lax.dynamic_index_in_dim(values, high, axis, keepdims=False),
            lax.dynamic_index_in_dim(values, 1 - high, axis, keepdims=False).astype(LOW),
        )

    def send(self):
        self.there = [
            over_planes(self.kept[m][1], self.left[m][0], self.planes) for m in range(2)
        ]

    def shrink(self):
        self.left = [left[1:] for left in self.left]

        def add(kept, there):
            return tuple(k[0].astype(FULL) + t.astype(FULL) for k, t in zip(kept, there))

        if self.left[0]:
            self.kept = self.line.run(lambda k, t: self.cut(add(k, t)), self.kept, self.there)
            self.send()
        else:
            self.part = (self.kept, self.there, add)

    def most(self):
        for _ in steps(self.planes)[1:]:
            self.shrink()

    def swap(self):
        core = lax.axis_index("core")

        def step(part):
            if isinstance(part, tuple):
                part = jnp.stack(part)
            part = part.astype(LOW)
            rows = part.shape[1] // 2
            return (
                lax.dynamic_slice_in_dim(part, core * rows, rows, 1),
                lax.dynamic_slice_in_dim(part, (1 - core) * rows, rows, 1),
            )

        if isinstance(self.part, tuple):
            kept, there, add = self.part
            self.keep, send = self.line.run(lambda k, t: step(add(k, t)), kept, there)
        else:
            self.keep, send = self.line.run(step, self.part)
        self.sibling = over("core", send)

    def hop(self):
        core, pair, _ = place()
        stays = core == pair
        self.own, send = self.line.run(
            lambda a, b: (jnp.where(stays, a, b), jnp.where(stays, b, a)), self.keep, self.sibling
        )
        self.other = over("zp", send)

    def cross(self):
        core = lax.axis_index("core")
        both = self.line.run(
            lambda a, b: jnp.where(core == 0, jnp.stack([a, b]), jnp.stack([b, a])),
            self.keep,
            self.sibling,
        )
        self.total = lax.psum_scatter(both, "zp", scatter_dimension=0, tiled=False)


def mm(equation, left, right):
    return jnp.einsum(equation, left, right, preferred_element_type=FULL)


def per_device(
    planes,
    image_in,
    text_in,
    condition,
    image_cot,
    text_cot,
    qkv_weight,
    qv_bias,
    proj_weight,
    proj_bias,
    up_weight,
    up_bias,
    down_weight,
    down_bias,
    mod_weight,
    mod_bias,
):
    micro, image, quarter = image_in.shape
    length = image + text_in.shape[1]
    rows = -(-length // 16) * 16
    both = range(micro)
    core, pair, near = place()
    stays = core == pair
    is_image = lax.broadcasted_iota(jnp.int32, (rows, 1), 0) < image
    line = Line()

    def own_quarter(bias):
        return rehome(bias.astype(FULL))

    def by_row(table):
        return jnp.where(is_image, table[0][None], table[1][None])

    def sums(values):
        values = values.astype(FULL)
        return jnp.stack([values[:image].sum(axis=0), values[image:].sum(axis=0)])

    def gather(own):
        other, far = over("zl", own), over("core", own)
        return own, other, far, over("core", other)

    def fold(parts):
        own, near, (own_there, near_there) = parts
        line.wait(own_there)
        send = line.run(
            lambda a, b: (a.astype(FULL) + b.astype(FULL)).astype(LOW), near, near_there
        )
        return own, own_there, over("zl", send)

    def total(part):
        return part[0].astype(FULL) + part[1].astype(FULL) + part[2].astype(FULL)

    def row_sums(first, second):
        return jnp.stack([first.sum(axis=1), (first * second).sum(axis=1)])

    def columns(totals):
        return totals[0][:, None] / D, totals[1][:, None] / D

    row_count = mod_weight.shape[1]
    shards = [
        qkv_weight.reshape(2, row_count, -1),
        proj_weight.transpose(0, 2, 1),
        up_weight,
        down_weight.transpose(0, 2, 1),
    ]
    qkv_way = WeightGather(line, shards[0], planes)

    cond_all = dp_gather(condition, planes)
    silu_all = jax.nn.silu(cond_all.astype(FULL)).astype(LOW)
    dp_index = lax.axis_index(("yx", "core"))
    silu_rows = lax.dynamic_slice_in_dim(silu_all, dp_index * row_count, row_count, 1)
    mod_terms = mm("bi,sicj->bscj", silu_rows, mod_weight)
    mod_local = dp_scatter_sum(mod_terms, planes) + mod_bias.astype(FULL)[None]
    modulation = rehome(mod_local)
    wide_modulation = group_gather(modulation[:, :, :2])
    qv_own, proj_own, up_own, down_own = [
        own_quarter(bias) for bias in (qv_bias, proj_bias, up_bias, down_bias)
    ]
    qkv_own = jnp.concatenate([qv_own[:, 0], jnp.zeros_like(qv_own[:, 0]), qv_own[:, 1]], 1)

    call = functools.partial(rows_call, image=image, rows=rows)
    dense = 2 * rows * D
    hidden = up_weight.shape[2]

    def qkv_step(s, pieces):
        return line.run(
            lambda a, b, c, d: call(
                qkv_kernel,
                "qkv",
                tiles=a,
                tables=[b, c, d],
                outs=[(D, LOW), (3 * quarter, LOW), (LANES, FULL)],
                flops=dense * 3 * quarter,
                scratch=[(D, LOW)],
            ),
            pieces,
            wide_modulation[s],
            qkv,
            qkv_own[:, None],
        )

    def parts_of(outs):
        own, near, own_theirs, near_theirs = outs
        far = over("core", near_theirs)
        return own, near, (over("core", own_theirs), far)

    def spread_step(name, value, weight):
        return parts_of(
            line.run(
                lambda a, b: call(
                    spread_kernel,
                    name,
                    tiles=[a],
                    tables=[b],
                    outs=[(quarter, LOW)] * 4,
                    flops=dense * value.shape[1],
                ),
                value,
                weight,
            )
        )

    def up_step(pieces):
        return line.run(
            lambda a, b, c: call(
                up_kernel,
                "up",
                tiles=a,
                tables=[b, c],
                outs=[(D, LOW), (hidden, FULL), (hidden, LOW)],
                flops=dense * hidden,
            ),
            pieces,
            up,
            up_own[:, None],
        )

    def gather_step(pieces):
        return line.run(
            lambda a: call(gather_kernel, "gather", tiles=a, tables=[], outs=[(D, LOW)], flops=0),
            pieces,
        )[0]

    def mlp_back_step(value, pre):
        grad, *outs = line.run(
            lambda a, b, c, d: call(
                mlp_back_kernel,
                "mlp_back",
                tiles=[a, b],
                tables=[c, d],
                outs=[(hidden, LOW)] + [(quarter, LOW)] * 4,
                flops=dense * hidden * 2,
            ),
            value,
            pre,
            up,
            down,
        )
        return grad, parts_of(outs)

    def proj_back_step(pieces):
        return line.run(
            lambda a, b: call(
                proj_back_kernel,
                "proj_back",
                tiles=a,
                tables=[b],
                outs=[(D, LOW), (quarter, LOW)],
                flops=dense * quarter,
            ),
            pieces,
            proj,
        )

    def grad_step(lefts, rights):
        return line.run(lambda a, b: weight_grad(image, a, b), tuple(lefts), tuple(rights))

    def middle_step(s, part):
        def step(part, x, mod, bias):
            branch = total(part) + by_row(bias)
            value = x.astype(FULL) + by_row(mod[:, 2]) * branch
            return row_sums(value, value), value, branch

        totals, value, branch = line.run(step, part, inputs[s], modulation[s], proj_own)
        return group_sum(totals), value, branch

    def second_norm(s, totals, value):
        def step(totals, value, mod):
            average, square = columns(totals)
            factor = lax.rsqrt(square - average * average + NORM_EPS)
            normed = (value - average) * factor
            shifted = (normed * (1.0 + by_row(mod[:, 4])) + by_row(mod[:, 3])).astype(LOW)
            return shifted, normed, factor

        shifted, normed, factor = line.run(step, totals, value, modulation[s])
        return gather(shifted), normed, factor

    def cot_step(s):
        def step(cot, mod):
            low = (by_row(mod[:, 5]) * cot.astype(FULL)).astype(LOW)
            return low, sums(low)

        low, bias = line.run(step, cotangents[s], modulation[s])
        return gather(low), bias

    def scaled_step(s, part, normed, which):
        def step(part, normed, mod):
            grad = total(part)
            scaled = grad * (1.0 + by_row(mod[:, which]))
            return row_sums(scaled, normed), scaled, sums(grad), sums(grad * normed)

        totals, scaled, shift, scale = line.run(step, part, normed, modulation[s])
        return group_sum(totals), scaled, shift, scale

    def middle_back(s, totals, scaled, normed, factor, branch):
        def step(totals, scaled, normed, factor, branch, cot, mod):
            grad_mean, cross_mean = columns(totals)
            grad = cot.astype(FULL) + factor * (scaled - grad_mean - normed * cross_mean)
            low = (by_row(mod[:, 2]) * grad).astype(LOW)
            return low, grad, sums(grad * branch), sums(low)

        low, grad, gate, bias = line.run(
            step, totals, scaled, normed, factor, branch, cotangents[s], modulation[s]
        )
        return gather(low), grad, gate, bias

    def first_back(totals, scaled, normed, stats, grad_middle):
        def step(totals, scaled, normed, stats, grad_middle):
            grad_mean, cross_mean = columns(totals)
            grad = grad_middle + stats[:, 1:2] * (scaled - grad_mean - normed * cross_mean)
            return grad.astype(LOW), grad

        low, grad = line.run(step, totals, scaled, normed, stats, grad_middle)
        return grad, away(low)

    def output_step(s, part, value):
        def step(part, value, cot, mod, bias):
            branch = total(part) + by_row(bias)
            out = (value + by_row(mod[:, 5]) * branch).astype(LOW)
            return out, sums(cot.astype(FULL) * branch)

        out, gate = line.run(step, part, value, cotangents[s], modulation[s], down_own)
        return (out, away(out)), gate

    def first_norm(s, stats):
        return line.run(
            lambda x, t: (x.astype(FULL) - t[:, 0:1]) * t[:, 1:2], inputs[s], stats
        )

    none = [None] * micro
    wide, attn_in, joint, stats, attended, log_total = (list(none) for _ in range(6))
    branch_one, middle, totals, normed_two, factor_two = (list(none) for _ in range(5))
    mlp_in, pre_act, activated, grad_two, grad_two_full = (list(none) for _ in range(5))
    grad_pre, part_a, part_b, part_c = (list(none) for _ in range(4))
    shift_two, scale_two, gate_two, shift_one, scale_one, gate_one = (list(none) for _ in range(6))
    scaled, grad_middle, one_bias, grad_one_full, grad_joint = (list(none) for _ in range(5))
    normed_one, outs, grad_in = (list(none) for _ in range(3))

    def settle_in(own, moved):
        return line.run(lambda a, b: jnp.where(stays, a, b), own, moved)

    two_bias, pieces, parts = list(none), list(none), list(none)

    raw = line.run(functools.partial(join, rows), image_in, text_in)
    qkv_way.swap()
    moved = away(after(raw[0], qkv_way.keep))
    qkv_way.split()
    line.wait(mod_local)
    inputs = [settle_in(raw[0], moved)]
    wide[0] = gather(inputs[0])
    proj_way = WeightGather(line, after(shards[1], inputs[0]), planes)
    qkv_way.most()
    proj_way.swap()
    up_way = WeightGather(line, after(shards[2], proj_way.keep), planes)
    proj_way.split()
    cot_raw = line.run(functools.partial(join, rows), image_cot, text_cot)
    line.wait(wide[0][1])
    qkv = qkv_way.grow()
    attn_in[0], joint[0], stats[0] = qkv_step(0, wide[0])
    up_way.swap()
    moved = away(after(raw[1], up_way.keep))
    up = up_way.offload()
    proj_way.most()
    attended[0], log_total[0] = line.run(lambda a: attend(a, length), joint[0])
    inputs.append(settle_in(raw[1], moved))
    wide[1] = gather(inputs[1])
    moved = away(after(cot_raw[0], inputs[1]))
    proj = proj_way.grow()
    part_a[0] = spread_step("proj", attended[0], proj)
    part_a[0] = fold(part_a[0])
    cotangents = [settle_in(cot_raw[0], moved)]
    down_way = WeightGather(line, after(shards[3], cotangents[0]), planes)
    attn_in[1], joint[1], stats[1] = qkv_step(1, wide[1])
    totals[0], middle[0], branch_one[0] = middle_step(0, part_a[0])
    attended[1], log_total[1] = line.run(lambda a: attend(a, length), joint[1])
    down_way.swap()
    down = down_way.offload()
    pieces[0], normed_two[0], factor_two[0] = second_norm(0, totals[0], middle[0])
    part_a[1] = spread_step("proj", attended[1], proj)
    normed_one[0] = first_norm(0, stats[0])
    normed_one[1] = first_norm(1, stats[1])
    line.wait(pieces[0][1])
    part_a[1] = fold(part_a[1])
    mlp_in[0], pre_act[0], activated[0] = up_step(pieces[0])
    totals[1], middle[1], branch_one[1] = middle_step(1, part_a[1])
    pieces[1], normed_two[1], factor_two[1] = second_norm(1, totals[1], middle[1])
    line.wait(pieces[1][1])
    grad_two[0], two_bias[0] = cot_step(0)
    moved = away(after(cot_raw[1], grad_two[0][0]))
    mlp_in[1], pre_act[1], activated[1] = up_step(pieces[1])
    cotangents.append(settle_in(cot_raw[1], moved))
    line.wait(grad_two[0][1])
    grad_two[1], two_bias[1] = cot_step(1)
    grad_two_full[0] = gather_step(grad_two[0])
    line.wait(grad_two[1][1])
    grad_two_full[1] = gather_step(grad_two[1])

    down_sum = WeightReduce(line, planes)
    down_sum.offload(grad_step(grad_two_full, activated)[0])
    grad_pre[0], part_b[0] = mlp_back_step(grad_two_full[0], pre_act[0])
    part_b[0] = fold(part_b[0])
    grad_pre[1], part_b[1] = mlp_back_step(grad_two_full[1], pre_act[1])
    totals[0], scaled[0], shift_two[0], scale_two[0] = scaled_step(0, part_b[0], normed_two[0], 4)
    up_sum = WeightReduce(line, planes)
    grad, up_rows = grad_step(mlp_in, grad_pre)
    up_sum.offload(grad)
    part_b[1] = fold(part_b[1])
    part_c[0] = spread_step("down", activated[0], down)
    pieces[0], grad_middle[0], gate_one[0], one_bias[0] = middle_back(
        0, totals[0], scaled[0], normed_two[0], factor_two[0], branch_one[0]
    )
    part_c[1] = spread_step("down", activated[1], down)
    line.wait(pieces[0][1])
    totals[1], scaled[1], shift_two[1], scale_two[1] = scaled_step(1, part_b[1], normed_two[1], 4)
    part_c[0] = fold(part_c[0])
    pieces[1], grad_middle[1], gate_one[1], one_bias[1] = middle_back(
        1, totals[1], scaled[1], normed_two[1], factor_two[1], branch_one[1]
    )
    down_sum.swap()
    grad_one_full[0], grad_attended = proj_back_step(pieces[0])
    outs[0], gate_two[0] = output_step(0, part_c[0], middle[0])
    part_c[1] = fold(part_c[1])
    down_sum.cross()
    grad_joint[0] = line.run(
        lambda a, b, c: attend_back(a, b, c, length), joint[0], log_total[0], grad_attended
    )
    up_sum.swap()
    grad_one_full[1], grad_attended = proj_back_step(pieces[1])
    up_sum.cross()
    part_a[0] = spread_step("qkv_back", grad_joint[0], qkv)
    proj_sum = WeightReduce(line, planes)
    proj_sum.offload(grad_step(grad_one_full, attended)[0])
    part_a[0] = fold(part_a[0])
    grad_joint[1] = line.run(
        lambda a, b, c: attend_back(a, b, c, length), joint[1], log_total[1], grad_attended
    )
    down_grad = line.run(lambda a: a.astype(FULL).transpose(0, 2, 1), down_sum.total)
    part_a[1] = spread_step("qkv_back", grad_joint[1], qkv)
    totals[0], scaled[0], shift_one[0], scale_one[0] = scaled_step(0, part_a[0], normed_one[0], 1)
    part_a[1] = fold(part_a[1])
    qkv_sum = WeightReduce(line, planes)
    grad, qkv_rows = grad_step(attn_in, grad_joint)
    qkv_sum.split(grad)
    grad_in[0] = first_back(totals[0], scaled[0], normed_one[0], stats[0], grad_middle[0])
    outs[1], gate_two[1] = output_step(1, part_c[1], middle[1])

    def pack():
        qv = jnp.concatenate([qkv_rows[:, 0, :quarter], qkv_rows[:, 0, 2 * quarter :]], 1)
        return jnp.concatenate(
            [qv, one_bias[0] + one_bias[1], two_bias[0] + two_bias[1], up_rows[:, 0]], 1
        )

    def mod_rows(s):
        return jnp.concatenate(
            [shift_one[s], scale_one[s], gate_one[s], shift_two[s], scale_two[s], gate_two[s]], 1
        )

    packed = line.run(pack)
    up_grad = line.run(lambda a: a.astype(FULL), up_sum.total)
    line.wait(grad_in[0][1])
    qkv_sum.most()
    totals[1], scaled[1], shift_one[1], scale_one[1] = scaled_step(1, part_a[1], normed_one[1], 1)
    proj_sum.swap()
    grad_in[1] = first_back(totals[1], scaled[1], normed_one[1], stats[1], grad_middle[1])
    grad_mods = line.run(lambda: jnp.stack([mod_rows(s) for s in both]).astype(LOW))
    line.wait(outs[1][1])
    grad_mods = line.run(rehome, grad_mods)
    qkv_sum.shrink()
    qkv_sum.swap()
    qkv_sum.hop()
    proj_sum.hop()

    def late(outs):
        outs = [jnp.where(stays, own, home) for own, home in outs]
        return (
            jnp.stack([out[:image] for out in outs]),
            jnp.stack([out[image:length] for out in outs]),
        )

    image_out, text_out = line.run(late, outs)

    def last_sums(grad_mods, packed, silu_rows, mod_weight, condition):
        every = dp_gather(grad_mods, planes)
        every = every.reshape(*every.shape[:2], 6, quarter)
        silu_grad = mm("bscj,sicj->bi", every, mod_weight)
        silu_grad = lax.all_to_all(
            silu_grad, ("yx", "core"), split_axis=0, concat_axis=1, tiled=True
        )
        for bit in steps(planes):
            packed = packed + over_planes(packed, bit, planes)
        packed = after(packed, silu_grad)
        packed = packed + over("zp", packed)
        packed = jnp.where(stays, packed, over("core", packed))
        silu_grad = silu_grad + over("zp", silu_grad)
        silu_grad = silu_grad + over("zl", silu_grad)
        return (
            jax.vjp(jax.nn.silu, condition.astype(FULL))[1](silu_grad)[0],
            mm("bi,bscj->sicj", silu_rows, every),
            jnp.sum(every.astype(FULL), axis=0),
            packed,
        )

    flag = condition[0, 0] == condition[0, 0]
    condition_grad, mod_weight_grad, mod_bias_grad, packed = line.run(
        functools.partial(apart, flag, last_sums),
        grad_mods,
        packed,
        silu_rows,
        mod_weight,
        condition,
    )
    qkv_grad, proj_grad = line.run(
        lambda sums: [own.astype(FULL) + other.astype(FULL) for own, other in sums],
        [(one.own, one.other) for one in (qkv_sum, proj_sum)],
    )
    qkv_grad = qkv_grad.reshape(qkv_weight.shape)
    bias_grads = [
        packed[:, : 2 * quarter].reshape(qv_bias.shape),
        packed[:, 2 * quarter : 3 * quarter],
        packed[:, 4 * quarter :],
        packed[:, 3 * quarter : 4 * quarter],
    ]

    grad_in = [jnp.where(stays, own, home.astype(FULL)) for own, home in grad_in]
    image_grad = jnp.stack([grad[:image] for grad in grad_in])
    text_grad = jnp.stack([grad[image:length] for grad in grad_in])
    proj_grad = proj_grad.transpose(0, 2, 1)
    return (
        image_out,
        text_out,
        image_grad,
        text_grad,
        condition_grad,
        qkv_grad,
        bias_grads[0],
        proj_grad,
        bias_grads[1],
        up_grad,
        bias_grads[2],
        down_grad,
        bias_grads[3],
        mod_weight_grad,
        mod_bias_grad,
    )


def solution(mesh):
    planes = mesh.shape["dp"] // 2
    split = Mesh(mesh.devices.reshape(planes, 2, 2, 2), ("yx", "core", "zp", "zl"))
    dp, tensor = ("yx", "core"), ("zp", "zl")
    tokens = P(dp, None, tensor)
    placed = (
        tokens,
        tokens,
        P(dp, None),
        tokens,
        tokens,
        P(None, dp, None, tensor),
        P(None, None, tensor),
        P(None, tensor, dp),
        P(None, tensor),
        P(None, dp, tensor),
        P(None, tensor),
        P(None, tensor, dp),
        P(None, tensor),
        P(None, dp, None, tensor),
        P(None, None, tensor),
    )
    return jax.shard_map(
        functools.partial(per_device, planes),
        mesh=split,
        in_specs=placed,
        out_specs=(tokens,) * 4 + (P(dp, None),) + placed[5:],
        check_vma=False,
    )
```
